256 devices in a mesh: chan: 64 (over x, y_hi, z), stn: 4 (over y_lo, core).
Axes of the slice: x: 4, y: 4 (y_hi: 2, y_lo: 2; y = y_hi * 2 + y_lo), z: 8, core: 2. Of those that a mesh axis runs over, the one named last changes fastest.
Arguments:
- gains: float32 [128, 2, 2, 2, 16, 512], P('chan', None, None, None, None, 'stn'), may hold values from -2.1 to 2.1
- coherency: bfloat16 [128, 16, 2, 512, 512], P('chan', None, None, 'stn'), may hold values from -1.5 to 1.5
- vis_data: bfloat16 [128, 2, 2, 2, 512, 512], P('chan', None, None, None, 'stn'), may hold values from -6 to 6
- flags: int32 [128, 32, 32], P('chan', 'stn'), may hold values 0 or 1
- beam: float32 [8, 16], replicated, may hold values from 0.5 to 2
- group_of: int32 [512], replicated, may hold values from 0 to 7
Outputs:
- gain_step: float32 [128, 2, 2, 2, 16, 512], P('chan', None, None, None, None, 'stn')
- loss_value: float32 [], replicated
The draws below stay inside these ranges and needn't reach their ends.
All inputs are finite; a program needn't handle non-finite values. No bound on the sum of `flags` on one device may be relied on, other than what follows from the above.
Results may differ from the reference program's by a relative error of at most 0.0003.
Values sent between devices are 32-bit elements; how exact they have to be, the bound alone decides.
No kernel may reach another device: no remote copies, remote signals or barrier semaphores. Data moves between devices by JAX's collectives and lax.ppermute only.
A program may use at most 128 MiB of HBM per device.

```python
import math
import jax
import jax.numpy as jnp
from jax import lax

K = 16
BLK = 16
NGRP = 8
S = 512
F = 128
NB = 32


def touch_ends(values, key, smallest, top_value):
    shape = values.shape
    place = [jax.random.randint(jax.random.fold_in(key, axis), (), 0, shape[axis]) for axis in range(len(shape))]
    values = values.at[tuple(place)].set(smallest)
    longest = shape.index(max(shape))
    place[longest] = (place[longest] + 1) % shape[longest]
    return values.at[tuple(place)].set(top_value)


def steps_of(own_key, shape, cuts, least, largest):
    gain, own = 1.0, jax.random.fold_in(own_key, 6)
    for axis_at, shards_of in cuts:
        heights = jnp.exp(jax.random.uniform(jax.random.fold_in(own, axis_at), (shards_of,), jnp.float32, least / len(cuts), largest / len(cuts)))
        gain = gain * jnp.repeat(heights, shape[axis_at] // shards_of).reshape([-1 if axis == axis_at else 1 for axis in range(len(shape))])
    return gain


def scatter_about(own_key, shape, scale, most, split=(), held_as=jnp.bfloat16):
    level = steps_of(own_key, shape, split, -0.22, 0.18) if split else 1.0
    array = jax.random.normal(own_key, shape, jnp.float32) * scale * level
    return jnp.minimum(jnp.maximum(array, -most), most).astype(held_as)


def setup_inputs(seed: int = 0) -> dict:
    key_list = jax.random.split(jax.random.key(seed), 7)
    return {
        "gains": scatter_about(key_list[0], (F, 2, 2, 2, K, S), 0.35, 2.1, ((0, 64), (5, 4)), jnp.float32),
        "coherency": scatter_about(key_list[1], (F, K, 2, S, S), 0.25, 1.5, ((0, 64), (3, 4))),
        "vis_data": scatter_about(key_list[2], (F, 2, 2, 2, S, S), 1.0, 6.0, ((0, 64), (4, 4))),
        "flags": touch_ends((jax.random.randint(key_list[3], (F, NB, NB), 0, 4) < 3).astype(jnp.int32), jax.random.fold_in(key_list[3], 1), 0, 1),
        "beam": jnp.clip(jnp.exp(jax.random.uniform(key_list[4], (NGRP, K), jnp.float32, math.log(0.5), math.log(2.0))), 0.5, 2.0),
        "group_of": touch_ends(jax.random.randint(key_list[5], (S,), 0, NGRP), jax.random.fold_in(key_list[5], 1), 0, NGRP - 1).astype(jnp.int32),
    }


smooth_weight = 0.05
damping = 0.3


def beam_factor(beam, group_of):
    groups = beam.shape[0]
    onehot = (group_of[None, :] == jnp.arange(groups, dtype=jnp.int32)[:, None]).astype(jnp.float32)
    return jnp.sum(beam[:, :, None] * onehot[:, None, :], axis=0)


def expand_flags(flags):
    chans, first, second = flags.shape
    wide = jnp.broadcast_to(flags.astype(jnp.float32)[:, :, None, :, None], (chans, first, BLK, second, BLK))
    return wide.reshape(chans, first * BLK, second * BLK)


def outer_product(row_dir, col_dir):
    row_real = row_dir[:, 0][:, :, None, :, :, None]
    row_imag = row_dir[:, 1][:, :, None, :, :, None]
    col_real = col_dir[:, 0][:, None, :, :, None, :]
    col_imag = col_dir[:, 1][:, None, :, :, None, :]
    real_part = jnp.sum(row_real * col_real + row_imag * col_imag, axis=3)
    imag_part = jnp.sum(row_imag * col_real - row_real * col_imag, axis=3)
    return real_part, imag_part


def block_terms(coherency, vis_data, weight, row_gains, col_gains):
    count_dirs = row_gains.shape[4]
    chans, row_total, col_total = weight.shape
    empty = jnp.zeros((chans, 2, 2, row_total, col_total), jnp.float32)

    def model_turn(state_pair, dir_index):
        coh_dir = lax.dynamic_index_in_dim(coherency, dir_index, 1, False).astype(jnp.float32)
        coh_real = coh_dir[:, 0][:, None, None]
        coh_imag = coh_dir[:, 1][:, None, None]
        row_dir = lax.dynamic_index_in_dim(row_gains, dir_index, 4, False)
        col_dir = lax.dynamic_index_in_dim(col_gains, dir_index, 4, False)
        outer_real, outer_imag = outer_product(row_dir, col_dir)
        model_real = state_pair[0] + coh_real * outer_real - coh_imag * outer_imag
        model_imag = state_pair[1] + coh_real * outer_imag + coh_imag * outer_real
        return (model_real, model_imag), None

    dir_list = jnp.arange(count_dirs, dtype=jnp.int32)
    (model_real, model_imag), _ = lax.scan(model_turn, (empty, empty), dir_list)
    observed = vis_data.astype(jnp.float32)
    res_real = weight[:, None, None] * (observed[:, 0] - model_real)
    res_imag = weight[:, None, None] * (observed[:, 1] - model_imag)
    total_sq = jnp.sum(res_real * res_real + res_imag * res_imag)
    wide_real = res_real[:, :, :, None]
    wide_imag = res_imag[:, :, :, None]

    def gradient_turn(state_dummy, dir_index):
        coh_dir = lax.dynamic_index_in_dim(coherency, dir_index, 1, False).astype(jnp.float32)
        coh_real = coh_dir[:, 0][:, None, None]
        coh_imag = coh_dir[:, 1][:, None, None]
        row_dir = lax.dynamic_index_in_dim(row_gains, dir_index, 4, False)
        col_dir = lax.dynamic_index_in_dim(col_gains, dir_index, 4, False)
        col_real = col_dir[:, 0][:, None, :, :, None, :]
        col_imag = col_dir[:, 1][:, None, :, :, None, :]
        prod_real = jnp.sum(wide_real * col_real - wide_imag * col_imag, axis=2)
        prod_imag = jnp.sum(wide_real * col_imag + wide_imag * col_real, axis=2)
        row_grad_real = -jnp.sum(coh_real * prod_real + coh_imag * prod_imag, axis=-1)
        row_grad_imag = -jnp.sum(coh_real * prod_imag - coh_imag * prod_real, axis=-1)
        row_real = row_dir[:, 0][:, :, None, :, :, None]
        row_imag = row_dir[:, 1][:, :, None, :, :, None]
        herm_real = jnp.sum(wide_real * row_real + wide_imag * row_imag, axis=1)
        herm_imag = jnp.sum(wide_real * row_imag - wide_imag * row_real, axis=1)
        col_grad_real = -jnp.sum(coh_real * herm_real - coh_imag * herm_imag, axis=-2)
        col_grad_imag = -jnp.sum(coh_real * herm_imag + coh_imag * herm_real, axis=-2)
        power = weight * (coh_dir[:, 0] * coh_dir[:, 0] + coh_dir[:, 1] * coh_dir[:, 1])
        col_norm = jnp.sum(col_dir * col_dir, axis=(1, 2, 3))
        row_norm = jnp.sum(row_dir * row_dir, axis=(1, 2, 3))
        row_curv = jnp.sum(power * col_norm[:, None, :], axis=-1)
        col_curv = jnp.sum(power * row_norm[:, :, None], axis=-2)
        row_grad = jnp.stack([row_grad_real, row_grad_imag], axis=1)
        col_grad = jnp.stack([col_grad_real, col_grad_imag], axis=1)
        return state_dummy, (row_grad, row_curv, col_grad, col_curv)

    _, stacked = lax.scan(gradient_turn, jnp.float32(0.0), dir_list)
    row_grad = jnp.moveaxis(stacked[0], 0, 4)
    row_curv = jnp.moveaxis(stacked[1], 0, 1)
    col_grad = jnp.moveaxis(stacked[2], 0, 4)
    col_curv = jnp.moveaxis(stacked[3], 0, 1)
    return total_sq, row_grad, row_curv, col_grad, col_curv


def reference(gains, coherency, vis_data, flags, beam, group_of):
    factor = beam_factor(beam, group_of)
    effective = gains * factor
    station_ids = jnp.arange(S, dtype=jnp.int32)
    off_diagonal = (station_ids[:, None] != station_ids[None, :]).astype(jnp.float32)

    def per_channel(channel_items):
        coh_one, data_one, flag_one, gain_one = channel_items
        weight = expand_flags(flag_one[None]) * off_diagonal[None]
        results = block_terms(coh_one[None], data_one[None], weight, gain_one[None], gain_one[None])
        return (results[0], jnp.sum(weight), results[1][0], results[2][0], results[3][0], results[4][0])

    sq_all, count_all, row_grad, row_curv, col_grad, col_curv = lax.map(
        per_channel, (coherency, vis_data, flags, effective))
    count = jnp.sum(count_all)
    total_sq = jnp.sum(sq_all)
    norm_scale = (F * S) / count
    second = gains[2:] - 2.0 * gains[1:-1] + gains[:-2]
    pad_spec = [(1, 1)] + [(0, 0)] * 5
    diff_full = jnp.pad(second, pad_spec)
    diff_pad = jnp.pad(diff_full, pad_spec)
    smooth_grad = diff_pad[:-2] - 2.0 * diff_pad[1:-1] + diff_pad[2:]
    gradient = norm_scale * factor * (row_grad + col_grad) + smooth_weight * smooth_grad
    curvature = norm_scale * factor * factor * (row_curv + col_curv) + damping
    gain_step = gradient / curvature[:, None, None, None]
    loss_value = (norm_scale * total_sq + smooth_weight * jnp.sum(second * second)) / (F * S)
    return gain_step, loss_value
```

```python
import jax
import jax.numpy as jnp
import numpy as np
from jax import lax
from jax.experimental import pallas as pl
from jax.experimental.pallas import tpu as pltpu
from jax.sharding import PartitionSpec as P


BF = jnp.bfloat16
F32 = jnp.float32
BLK = 16
CHAN = "chan"
STN = "stn"
ALL = ("chan", "stn")
smooth_weight = 0.05
damping = 0.3


def selections():
    sel_w = np.zeros((64, 16), np.float32)
    sel_l = np.zeros((2, 16, 16), np.float32)
    for s in range(2):
        for t in range(2):
            for i in range(2):
                for r in range(2):
                    kk = ((s * 2 + t) * 2 + i) * 2 + r
                    for a in range(2):
                        sel_l[a, s * 8 + r * 4 + a * 2 + i, kk] = 1.0
                        sel_w[a * 16 + kk, t * 8 + r * 4 + a * 2 + i] = 1.0
                        sel_w[32 + a * 16 + kk, t * 8 + (1 - r) * 4 + a * 2 + i] = -1.0 if r == 0 else 1.0
    sel_c = np.zeros((2, 16, 16), np.float32)
    sel_q = np.zeros((4, 16, 16), np.float32)
    for s in range(2):
        for a in range(2):
            for i in range(2):
                re, im = s * 8 + a * 2 + i, s * 8 + 4 + a * 2 + i
                sel_c[a, s * 8 + i, re] = -1.0
                sel_c[a, s * 8 + 2 + i, im] = -1.0
                sel_c[a, s * 8 + 4 + i, im] = -1.0
                sel_c[a, s * 8 + 6 + i, re] = 1.0
                for half in range(2):
                    row = s * 8 + half * 4 + i
                    sel_q[a * 2, row, re] = -1.0
                    sel_q[a * 2, row + 2, im] = -1.0
                    sel_q[a * 2 + 1, row, im] = 1.0
                    sel_q[a * 2 + 1, row + 2, re] = -1.0
    w2 = np.concatenate([sel_w, sel_q.reshape(64, 16)], axis=0)
    return w2, sel_l, sel_c.reshape(32, 16)


def dot(a, b):
    return jnp.dot(a, b, preferred_element_type=F32)


def dot_t(a, b):
    return lax.dot_general(a, b, (((1,), (1,)), ((), ())), preferred_element_type=F32)


def dot_l(a, b):
    return lax.dot_general(a, b, (((0,), (0,)), ((), ())), preferred_element_type=F32)


def split(x):
    high = x.astype(BF)
    return high, (x - high.astype(F32)).astype(BF)


def parts_of(x):
    high = x.astype(BF).astype(F32)
    return jnp.concatenate([high, x - high], axis=0).astype(BF)


K = 16
ROWS = 128
LANES = 128
TILES = ROWS // 16


def weights_of(first, flags, wgt, groups):
    blocks, cols = flags.shape
    rows8 = lax.broadcasted_iota(jnp.int32, (ROWS, blocks), 0) // 16 == lax.broadcasted_iota(jnp.int32, (ROWS, blocks), 1)
    wide = dot(rows8.astype(F32).astype(BF), flags.astype(F32).astype(BF)).astype(BF)
    for g in range(groups):
        at = (lax.broadcasted_iota(jnp.int32, (cols, LANES), 1) + g * LANES) // 16
        at = at == lax.broadcasted_iota(jnp.int32, (cols, LANES), 0)
        full = dot(wide, at.astype(F32).astype(BF))
        row_id = lax.broadcasted_iota(jnp.int32, (ROWS, LANES), 0) + first
        col_id = lax.broadcasted_iota(jnp.int32, (ROWS, LANES), 1) + g * LANES
        wgt[:, g * LANES:(g + 1) * LANES] = jnp.where(row_id == col_id, 0.0, full)


def model_operands(f, jall, jrow, w2, sell, wr, wi, lr):
    groups = jall.shape[0]

    def turn(k, _):
        for g in range(groups):
            w = dot(w2[0:64], parts_of(jall[g, f, pl.ds(k, 8, stride=16), :])).astype(BF)
            for b in range(2):
                wr[k, g, :, b * 128:(b + 1) * 128] = w[b * 16:(b + 1) * 16]
                wi[k, g, :, b * 128:(b + 1) * 128] = w[32 + b * 16:48 + b * 16]
        hm = parts_of(jrow[f, pl.ds(k, 8, stride=16), :])
        for a in range(2):
            l = dot_l(hm, sell[a]).astype(BF)
            for t in range(TILES):
                lr[k, t, a * 16:(a + 1) * 16, :] = l[t * 16:(t + 1) * 16]
        return 0

    lax.fori_loop(0, K, turn, 0)


def model(f, coh, vis, wgt, res, wr, wi, lr, groups):
    def turn(t, sq):
        rows = pl.ds(pl.multiple_of(t * 16, 16), 16)
        for g in range(groups):
            cols = slice(g * 128, (g + 1) * 128)
            acc = [[[jnp.zeros((16, 128), F32)] * 2 for _ in range(2)] for _ in range(2)]
            for k in range(K):
                o_re = dot(lr[k, t], wr[k, g])
                o_im = dot(lr[k, t], wi[k, g])
                c_re = coh[f, k, 0, rows, cols].astype(F32)
                c_im = coh[f, k, 1, rows, cols].astype(F32)
                for a in range(2):
                    for b in range(2):
                        re = o_re[a * 16:(a + 1) * 16, b * 128:(b + 1) * 128]
                        im = o_im[a * 16:(a + 1) * 16, b * 128:(b + 1) * 128]
                        acc[a][b] = [acc[a][b][0] + c_re * re - c_im * im,
                                     acc[a][b][1] + c_re * im + c_im * re]
            w = wgt[rows, cols]
            for a in range(2):
                for b in range(2):
                    for r in range(2):
                        v = w * (vis[f, r, a, b, rows, cols].astype(F32) - acc[a][b][r])
                        res[b, r, pl.ds(pl.multiple_of(a * ROWS + t * 16, 16), 16), cols] = v
                        sq = sq + v * v
        return sq

    sq = lax.fori_loop(0, TILES, turn, jnp.zeros((16, 128), F32))
    return sq[:8] + sq[8:]


def norms(x):
    return parts_of(jnp.broadcast_to(jnp.sum(x * x, axis=0, keepdims=True), (8, LANES)))


def gradient_operands(f, jall, jrow, w2, selc, lq, lc, nq, nr):
    groups = jall.shape[0]
    span = groups * LANES

    def turn(k, _):
        for g in range(groups):
            x = jall[g, f, pl.ds(k, 8, stride=16), :]
            w = dot(w2[64:128], parts_of(x)).astype(BF)
            for j in range(4):
                lq[k, :, j * span + g * 128:j * span + (g + 1) * 128] = w[j * 16:j * 16 + 16]
            nq[k, :, g * 128:(g + 1) * 128] = norms(x)
        x = jrow[f, pl.ds(k, 8, stride=16), :]
        c = dot(selc[...], parts_of(x)).astype(BF)
        for a in range(2):
            lc[k, :, a * 128:(a + 1) * 128] = c[a * 16:(a + 1) * 16]
        nr[k] = norms(x)
        return 0

    lax.fori_loop(0, K, turn, 0)


def gradient(f, coh, wgt, res, lq, lc, nq, nr, bufs, row, col, groups):
    span = groups * LANES
    halves = groups // 2

    def fill(k, t, h, y, am):
        cols = slice(h * 256, (h + 1) * 256)
        rows = slice(t * 16, (t + 1) * 16)
        c_re = coh[f, k, 0, rows, cols].astype(F32)
        c_im = coh[f, k, 1, rows, cols].astype(F32)
        for a in range(2):
            at = slice(a * ROWS + t * 16, a * ROWS + t * 16 + 16)
            for b in range(2):
                r_re = res[b, 0, at, cols]
                r_im = res[b, 1, at, cols]
                for r, v in ((0, c_re * r_re + c_im * r_im), (1, c_re * r_im - c_im * r_re)):
                    high, low = split(v)
                    y[b * 2 + r, h, 0, at, :] = high
                    y[b * 2 + r, h, 1, at, :] = low
        high, low = split(wgt[rows, cols] * (c_re * c_re + c_im * c_im))
        am[h, rows, :] = high
        am[h, ROWS + t * 16:ROWS + t * 16 + 16, :] = low

    top = lax.broadcasted_iota(jnp.int32, (8, 128), 0) < 4

    def reduce_part(k, j, h, s, y, cell):
        tile = y[j, h, s]
        c = dot(lc[k], tile)
        r = dot_t(lq[k, :, j * span + h * 256:j * span + (h + 1) * 256], tile)
        c = c[:8] + c[8:]
        cell[0][j, h] = c if s == 0 else cell[0][j, h] + c
        cell[1] = r if cell[1] is None else cell[1] + r

    def reduce_end(k, am, cell):
        r = cell[1][:8] + cell[1][8:]
        row[pl.ds(k, 8, stride=16), :] = jnp.where(top, r[:, :ROWS], r[:, ROWS:])
        for g in range(groups):
            h, cols = g // 2, slice(g % 2 * 128, g % 2 * 128 + 128)
            c = [cell[0][j, h][:, cols] for j in range(4)]
            t0 = c[0] + pltpu.roll(c[1], 4, 0)
            t1 = pltpu.roll(c[2], 4, 0) + c[3]
            col[g, pl.ds(k, 8, stride=16), :] = jnp.where(top, t0, t1)
        total = None
        n_row = jnp.concatenate([nr[k], nr[k]], axis=1)
        for h in range(halves):
            tile = am[h]
            cc = dot(n_row, tile)
            cc = cc[0:1] + cc[8:9]
            for g in range(2):
                col[h * 2 + g, pl.ds(128 + k, 1), :] = cc[:, g * 128:(g + 1) * 128]
            cr = dot_t(nq[k, :, h * 256:(h + 1) * 256], tile)
            cr = cr[0:1] + cr[8:9]
            cr = cr[:, :ROWS] + cr[:, ROWS:]
            total = cr if total is None else total + cr
        row[pl.ds(128 + k, 1), :] = total

    fills = [(t, h) for t in range(TILES) for h in range(halves)]
    dots = [(j, h, s) for j in range(4) for h in range(halves) for s in range(2)]
    (y0, a0), (y1, a1) = bufs
    for t, h in fills:
        fill(0, t, h, y0, a0)

    def pair(i, _):
        for step, (y, am, y_next, am_next) in enumerate(((y0, a0, y1, a1), (y1, a1, y0, a0))):
            k = 2 * i + step
            k_next = jnp.minimum(k + 1, K - 1)
            cell = [{}, None]
            for (t, h), part in zip(fills, dots):
                reduce_part(k, *part, y, cell)
                fill(k_next, t, h, y_next, am_next)
            reduce_end(k, am, cell)
        return 0

    lax.fori_loop(0, K // 2, pair, 0)


def operand_scratch(G):
    S = G * 128
    return dict(
        model=[pltpu.VMEM((K, G, 16, 256), BF), pltpu.VMEM((K, G, 16, 256), BF), pltpu.VMEM((K, TILES, 32, 16), BF)],
        grad=[pltpu.VMEM((K, 16, 4 * S), BF), pltpu.VMEM((K, 16, 2 * ROWS), BF), pltpu.VMEM((K, 16, S), BF), pltpu.VMEM((K, 16, ROWS), BF)],
        bufs=[pltpu.VMEM((4, G // 2, 2, 2 * ROWS, 256), BF), pltpu.VMEM((G // 2, 2 * ROWS, 256), BF)] * 2,
    )


def front(first, jall, jrow, coh, vis, flags, w2, sell, selc, row, col, res1, wgt1, sq, res0, wgt0, wr, wi, lr, lq, lc, nq, nr, y0, a0, y1, a1):
    G = jall.shape[0]
    total = None
    for f, (res, wgt) in enumerate(((res0, wgt0), (res1, wgt1))):
        weights_of(first[0], flags[f], wgt, G)
        model_operands(f, jall, jrow, w2, sell, wr, wi, lr)
        part = model(f, coh, vis, wgt, res, wr, wi, lr, G)
        total = part if total is None else total + part
    sq[...] = total
    gradient_operands(0, jall, jrow, w2, selc, lq, lc, nq, nr)
    gradient(0, coh, wgt0, res0, lq, lc, nq, nr, ((y0, a0), (y1, a1)), row, col, G)


def back(jall, jrow, coh, res, wgt, w2, selc, row, col, lq, lc, nq, nr, y0, a0, y1, a1):
    G = jall.shape[0]
    gradient_operands(1, jall, jrow, w2, selc, lq, lc, nq, nr)
    gradient(0, coh, wgt, res, lq, lc, nq, nr, ((y0, a0), (y1, a1)), row, col, G)


def whole(x):
    return pl.BlockSpec(x.shape, lambda i: (0,) * x.ndim)


def spec(shape):
    return pl.BlockSpec(shape, lambda i: (0,) * len(shape))


def call_front(first, jall, jrow, coh, vis, flags, sels):
    G = jall.shape[0]
    S = G * 128
    sc = operand_scratch(G)
    outs = [(144, ROWS), (G, 144, ROWS), (2, 2, 2 * ROWS, S), (ROWS, S), (8, 128)]
    return pl.pallas_call(
        front, grid=(1,),
        out_shape=[jax.ShapeDtypeStruct(s, F32) for s in outs],
        in_specs=[pl.BlockSpec(memory_space=pltpu.SMEM)] + [whole(x) for x in (jall, jrow, coh, vis, flags, *sels)],
        out_specs=[spec(s) for s in outs],
        scratch_shapes=[pltpu.VMEM((2, 2, 2 * ROWS, S), F32), pltpu.VMEM((ROWS, S), F32), *sc["model"], *sc["grad"], *sc["bufs"]],
        cost_estimate=pl.CostEstimate(flops=40_000_000_000, bytes_accessed=20_000_000, transcendentals=0),
        name="front",
    )(first, jall, jrow, coh, vis, flags, *sels)


def call_back(jall, jrow, coh, res, wgt, sels):
    G = jall.shape[0]
    sc = operand_scratch(G)
    outs = [(144, ROWS), (G, 144, ROWS)]
    sels = (sels[0], sels[2])
    return pl.pallas_call(
        back, grid=(1,),
        out_shape=[jax.ShapeDtypeStruct(s, F32) for s in outs],
        in_specs=[whole(jall), whole(jrow), pl.BlockSpec((1, *coh.shape[1:]), lambda i: (1, 0, 0, 0, 0))] + [whole(x) for x in (res, wgt, *sels)],
        out_specs=[spec(s) for s in outs],
        scratch_shapes=[*sc["grad"], *sc["bufs"]],
        cost_estimate=pl.CostEstimate(flops=20_000_000_000, bytes_accessed=10_000_000, transcendentals=0),
        name="back",
    )(jall, jrow, coh, res, wgt, *sels)


def beam_factor(beam, group_of):
    groups = beam.shape[0]
    onehot = (group_of[None, :] == jnp.arange(groups, dtype=jnp.int32)[:, None]).astype(F32)
    return jnp.sum(beam[:, :, None] * onehot[:, None, :], axis=0)


def exchange(parts, axis):
    return lax.all_to_all(parts, axis, 0, 0, tiled=True)


def owned_sum(parts):
    count = parts.shape[0]
    me = lax.axis_index(STN)
    total = lax.dynamic_index_in_dim(parts, me, 0, False)
    for hop in range(1, count):
        part = lax.dynamic_index_in_dim(parts, lax.rem(me + hop, count), 0, False)
        total = total + lax.ppermute(part, STN, [(i, (i + hop) % count) for i in range(count)])
    return total


def on_device(gains, coherency, vis_data, flags, beam, group_of):
    chan_dev = gains.shape[0]
    row_count = gains.shape[5]
    stn_count = lax.axis_size(STN)
    chan_count = lax.axis_size(CHAN)
    first_row = lax.axis_index(STN) * row_count
    all_channels = chan_dev * chan_count
    all_stations = row_count * stn_count

    row_factor = lax.dynamic_slice_in_dim(beam_factor(beam, group_of), first_row, row_count, 1)
    own = (gains * row_factor).reshape(chan_dev, 8 * K, row_count)
    every = exchange(jnp.broadcast_to(own, (stn_count, *own.shape)), STN)

    up = [(i, i + 1) for i in range(chan_count - 1)]
    down = [(i + 1, i) for i in range(chan_count - 1)]
    extended = jnp.concatenate([lax.ppermute(gains, CHAN, up), gains, lax.ppermute(gains, CHAN, down)], axis=0)
    second = extended[2:] - 2.0 * extended[1:-1] + extended[:-2]
    positions = lax.axis_index(CHAN) * chan_dev - 1 + jnp.arange(chan_dev + 2, dtype=jnp.int32)
    inside = ((positions >= 1) & (positions <= all_channels - 2)).astype(F32)
    second = second * inside[:, None, None, None, None, None]
    smooth_grad = second[:-2] - 2.0 * second[1:-1] + second[2:]
    own_second = second[1:-1]
    smooth_local = jnp.sum(own_second * own_second)

    blocks = jnp.arange(flags.shape[1], dtype=jnp.int32) + first_row // BLK
    selves = blocks[:, None] == jnp.arange(flags.shape[2], dtype=jnp.int32)[None, :]
    local_count = jnp.sum(flags * jnp.where(selves, BLK * (BLK - 1), BLK * BLK)[None]).astype(F32)

    sels = tuple(jnp.asarray(x, BF) for x in selections())
    row0, col0, res, wgt, sq = call_front(first_row[None].astype(jnp.int32), every, own, coherency, vis_data, flags, sels)
    lane = jnp.arange(row_count)
    packed = jnp.where(lane == 0, local_count, jnp.where(lane == 1, jnp.sum(sq), jnp.where(lane == 2, smooth_local, 0.0)))
    devices = chan_count * stn_count
    packed, own_back = lax.optimization_barrier((packed, own))
    arrived = exchange(jnp.broadcast_to(packed, (devices, row_count)), ALL)
    got0 = owned_sum(col0)
    row1, col1 = call_back(every, own_back, coherency, res, wgt, sels)
    col1, arrived = lax.optimization_barrier((col1, arrived))
    got1 = jnp.sum(exchange(col1, STN), axis=0)
    totals = jnp.sum(arrived, axis=0)

    norm_scale = all_channels * all_stations / totals[0]
    steps = []
    for f, (row, got) in enumerate(((row0, got0), (row1, got1))):
        both = row + got
        grad = both[:8 * K].reshape(2, 2, 2, K, row_count).swapaxes(0, 1)
        curv = both[8 * K:]
        gradient = norm_scale * row_factor * grad + smooth_weight * smooth_grad[f]
        curvature = norm_scale * row_factor * row_factor * curv + damping
        steps.append(gradient / curvature)
    gain_step = jnp.stack(steps)
    loss_value = (norm_scale * totals[1] + smooth_weight * totals[2]) / (all_channels * all_stations)
    return gain_step, loss_value


def solution(mesh):
    in_specs = (
        P(CHAN, None, None, None, None, STN),
        P(CHAN, None, None, STN, None),
        P(CHAN, None, None, None, STN, None),
        P(CHAN, STN, None),
        P(),
        P(),
    )
    out_specs = (P(CHAN, None, None, None, None, STN), P())

    return jax.shard_map(on_device, mesh=mesh, in_specs=in_specs, out_specs=out_specs, check_vma=False)
```

```python
import functools

import jax
import jax.numpy as jnp
import numpy as np
from jax import lax
from jax.experimental import pallas as pl
from jax.experimental.pallas import tpu as pltpu
from jax.sharding import Mesh
from jax.sharding import PartitionSpec as P


BF = jnp.bfloat16
F32 = jnp.float32
BLK = 16
CHAN = ("chan_x", "chan_y", "chan_z")
STN = "stn"
NEAR = ("chan_x", "stn")
OUTER = ("chan_y", "chan_z")
smooth_weight = 0.05
damping = 0.3


def selections():
    sel_w = np.zeros((64, 16), np.float32)
    sel_l = np.zeros((2, 16, 16), np.float32)
    for s in range(2):
        for t in range(2):
            for i in range(2):
                for r in range(2):
                    kk = ((s * 2 + t) * 2 + i) * 2 + r
                    for a in range(2):
                        sel_l[a, s * 8 + r * 4 + a * 2 + i, kk] = 1.0
                        sel_w[a * 16 + kk, t * 8 + r * 4 + a * 2 + i] = 1.0
                        sel_w[32 + a * 16 + kk, t * 8 + (1 - r) * 4 + a * 2 + i] = -1.0 if r == 0 else 1.0
    sel_c = np.zeros((2, 16, 16), np.float32)
    sel_q = np.zeros((4, 16, 16), np.float32)
    for s in range(2):
        for a in range(2):
            for i in range(2):
                re, im = s * 8 + a * 2 + i, s * 8 + 4 + a * 2 + i
                sel_c[a, s * 8 + i, re] = -1.0
                sel_c[a, s * 8 + 2 + i, im] = -1.0
                sel_c[a, s * 8 + 4 + i, im] = -1.0
                sel_c[a, s * 8 + 6 + i, re] = 1.0
                for half in range(2):
                    row = s * 8 + half * 4 + i
                    sel_q[a * 2, row, re] = -1.0
                    sel_q[a * 2, row + 2, im] = -1.0
                    sel_q[a * 2 + 1, row, im] = 1.0
                    sel_q[a * 2 + 1, row + 2, re] = -1.0
    w2 = np.concatenate([sel_w, sel_q.reshape(64, 16)], axis=0)
    return w2, sel_l, sel_c.reshape(32, 16)


def dot(a, b):
    return jnp.dot(a, b, preferred_element_type=F32)


def dot_t(a, b):
    return lax.dot_general(a, b, (((1,), (1,)), ((), ())), preferred_element_type=F32)


def dot_l(a, b):
    return lax.dot_general(a, b, (((0,), (0,)), ((), ())), preferred_element_type=F32)


def split(x):
    high = x.astype(BF)
    return high, (x - high.astype(F32)).astype(BF)


def parts_of(x):
    high = x.astype(BF).astype(F32)
    return jnp.concatenate([high, x - high], axis=0).astype(BF)


K = 16
ROWS = 128
LANES = 128
TILES = ROWS // 16


def weights_of(first, flags, wgt, groups):
    blocks, cols = flags.shape
    rows8 = lax.broadcasted_iota(jnp.int32, (ROWS, blocks), 0) // 16 == lax.broadcasted_iota(jnp.int32, (ROWS, blocks), 1)
    wide = dot(rows8.astype(F32).astype(BF), flags.astype(F32).astype(BF)).astype(BF)
    for g in range(groups):
        at = (lax.broadcasted_iota(jnp.int32, (cols, LANES), 1) + g * LANES) // 16
        at = at == lax.broadcasted_iota(jnp.int32, (cols, LANES), 0)
        full = dot(wide, at.astype(F32).astype(BF))
        row_id = lax.broadcasted_iota(jnp.int32, (ROWS, LANES), 0) + first
        col_id = lax.broadcasted_iota(jnp.int32, (ROWS, LANES), 1) + g * LANES
        wgt[:, g * LANES:(g + 1) * LANES] = jnp.where(row_id == col_id, 0.0, full)


def model_operands(jall, me, w2, sell, wr, wi, lr):
    groups = jall.shape[0]

    def turn(k, _):
        for g in range(groups):
            w = dot(w2[0:64], parts_of(jall[g, pl.ds(k, 8, stride=16), :])).astype(BF)
            for b in range(2):
                wr[k, g, :, b * 128:(b + 1) * 128] = w[b * 16:(b + 1) * 16]
                wi[k, g, :, b * 128:(b + 1) * 128] = w[32 + b * 16:48 + b * 16]
        hm = parts_of(jall[me, pl.ds(k, 8, stride=16), :])
        for a in range(2):
            l = dot_l(hm, sell[a]).astype(BF)
            for t in range(TILES):
                lr[k, t, a * 16:(a + 1) * 16, :] = l[t * 16:(t + 1) * 16]
        return 0

    lax.fori_loop(0, K, turn, 0)


def model(me_ref, own, mate, over, far, factor, coh, vis, flags, w2, sell, jall, res, wgt, sq, w_all, wr, wi, lr):
    groups = jall.shape[0]
    t = pl.program_id(0)
    me = me_ref[0]

    @pl.when(t == 0)
    def _():
        for hop, piece in enumerate((own, mate, over, far)):
            g = me ^ hop
            scale = factor[g]
            for plane in range(8):
                at = slice(plane * K, (plane + 1) * K)
                jall[g, at, :] = piece[0, at, :] * scale
        weights_of(me * ROWS, flags[0], w_all, groups)
        model_operands(jall, me, w2, sell, wr, wi, lr)
        sq[...] = jnp.zeros_like(sq)

    w_rows = w_all[pl.ds(pl.multiple_of(t * 16, 16), 16), :]
    wgt[...] = w_rows
    total = jnp.zeros((16, 128), F32)
    for g in range(groups):
        cols = slice(g * 128, (g + 1) * 128)
        acc = [[[jnp.zeros((16, 128), F32)] * 2 for _ in range(2)] for _ in range(2)]
        for k in range(K):
            o_re = dot(lr[k, t], wr[k, g])
            o_im = dot(lr[k, t], wi[k, g])
            c_re = coh[0, k, 0, :, cols].astype(F32)
            c_im = coh[0, k, 1, :, cols].astype(F32)
            for a in range(2):
                for b in range(2):
                    re = o_re[a * 16:(a + 1) * 16, b * 128:(b + 1) * 128]
                    im = o_im[a * 16:(a + 1) * 16, b * 128:(b + 1) * 128]
                    acc[a][b] = [acc[a][b][0] + c_re * re - c_im * im,
                                 acc[a][b][1] + c_re * im + c_im * re]
        w = w_rows[:, cols]
        for a in range(2):
            for b in range(2):
                for r in range(2):
                    v = w * (vis[0, r, a, b, :, cols].astype(F32) - acc[a][b][r])
                    res[b, r, a, :, cols] = v
                    total = total + v * v
    sq[...] += total[:8] + total[8:]


def norms(x):
    return parts_of(jnp.broadcast_to(jnp.sum(x * x, axis=0, keepdims=True), (8, LANES)))


def gradient_operands(jall, me, w2, selc, lq, lc, nq, nr):
    groups = jall.shape[0]
    span = groups * LANES

    def turn(k, _):
        for g in range(groups):
            x = jall[g, pl.ds(k, 8, stride=16), :]
            w = dot(w2[64:128], parts_of(x)).astype(BF)
            for j in range(4):
                lq[k, :, j * span + g * 128:j * span + (g + 1) * 128] = w[j * 16:j * 16 + 16]
            nq[k, :, g * 128:(g + 1) * 128] = norms(x)
        x = jall[me, pl.ds(k, 8, stride=16), :]
        c = dot(selc[...], parts_of(x)).astype(BF)
        for a in range(2):
            lc[k, :, a * 128:(a + 1) * 128] = c[a * 16:(a + 1) * 16]
        nr[k] = norms(x)
        return 0

    lax.fori_loop(0, K, turn, 0)


def gradient(coh, wgt, res, lq, lc, nq, nr, bufs, row, col, groups, rest):
    span = groups * LANES
    halves = groups // 2

    def fill(k, t, h, y, am):
        cols = slice(h * 256, (h + 1) * 256)
        rows = slice(t * 16, (t + 1) * 16)
        c_re = coh[k, 0, rows, cols].astype(F32)
        c_im = coh[k, 1, rows, cols].astype(F32)
        for a in range(2):
            at = slice(a * ROWS + t * 16, a * ROWS + t * 16 + 16)
            for b in range(2):
                r_re = res[b, 0, a, rows, cols]
                r_im = res[b, 1, a, rows, cols]
                for r, v in ((0, c_re * r_re + c_im * r_im), (1, c_re * r_im - c_im * r_re)):
                    high, low = split(v)
                    y[b * 2 + r, h, 0, at, :] = high
                    y[b * 2 + r, h, 1, at, :] = low
        high, low = split(wgt[rows, cols] * (c_re * c_re + c_im * c_im))
        am[h, rows, :] = high
        am[h, ROWS + t * 16:ROWS + t * 16 + 16, :] = low

    top = lax.broadcasted_iota(jnp.int32, (8, 128), 0) < 4

    def reduce_part(k, j, h, s, y, cell):
        tile = y[j, h, s]
        c = dot(lc[k], tile)
        r = dot_t(lq[k, :, j * span + h * 256:j * span + (h + 1) * 256], tile)
        c = c[:8] + c[8:]
        cell[0][j, h] = c if s == 0 else cell[0][j, h] + c
        cell[1] = r if cell[1] is None else cell[1] + r

    def reduce_end(k, am, cell):
        r = cell[1][:8] + cell[1][8:]
        row[pl.ds(k, 8, stride=16), :] = jnp.where(top, r[:, :ROWS], r[:, ROWS:])
        for g in range(groups):
            h, cols = g // 2, slice(g % 2 * 128, g % 2 * 128 + 128)
            c = [cell[0][j, h][:, cols] for j in range(4)]
            t0 = c[0] + pltpu.roll(c[1], 4, 0)
            t1 = pltpu.roll(c[2], 4, 0) + c[3]
            col[g, pl.ds(k, 8, stride=16), :] = jnp.where(top, t0, t1)
        total = None
        n_row = jnp.concatenate([nr[k], nr[k]], axis=1)
        for h in range(halves):
            tile = am[h]
            cc = dot(n_row, tile)
            cc = cc[0:1] + cc[8:9]
            for g in range(2):
                col[h * 2 + g, pl.ds(128 + k, 1), :] = cc[:, g * 128:(g + 1) * 128]
            cr = dot_t(nq[k, :, h * 256:(h + 1) * 256], tile)
            cr = cr[0:1] + cr[8:9]
            cr = cr[:, :ROWS] + cr[:, ROWS:]
            total = cr if total is None else total + cr
        row[pl.ds(128 + k, 1), :] = total

    fills = [(t, h) for t in range(TILES) for h in range(halves)]
    dots = [(j, h, s) for j in range(4) for h in range(halves) for s in range(2)]
    (y0, a0), (y1, a1) = bufs
    for t, h in fills:
        fill(0, t, h, y0, a0)
    rest()

    def pair(i, _):
        for step, (y, am, y_next, am_next) in enumerate(((y0, a0, y1, a1), (y1, a1, y0, a0))):
            k = 2 * i + step
            k_next = jnp.minimum(k + 1, K - 1)
            cell = [{}, None]
            for (t, h), part in zip(fills, dots):
                reduce_part(k, *part, y, cell)
                fill(k_next, t, h, y_next, am_next)
            reduce_end(k, am, cell)
        return 0

    lax.fori_loop(0, K // 2, pair, 0)


def operand_scratch(G):
    S = G * 128
    return dict(
        model=[pltpu.VMEM((K, G, 16, 256), BF), pltpu.VMEM((K, G, 16, 256), BF), pltpu.VMEM((K, TILES, 32, 16), BF)],
        grad=[pltpu.VMEM((K, 16, 4 * S), BF), pltpu.VMEM((K, 16, 2 * ROWS), BF), pltpu.VMEM((K, 16, S), BF), pltpu.VMEM((K, 16, ROWS), BF)],
        bufs=[pltpu.VMEM((4, G // 2, 2, 2 * ROWS, 256), BF), pltpu.VMEM((G // 2, 2 * ROWS, 256), BF)] * 2,
    )


def grad_kernel(f, me_ref, jall, coh_hbm, res_hbm, wgt, w2, selc, row, col0, col1, col2, col3,
                coh, res, sems, col, lq, lc, nq, nr, y0, a0, y1, a1):
    groups = jall.shape[0]
    me = me_ref[0]
    load_res = pltpu.make_async_copy(res_hbm, res, sems.at[0])
    load_first = pltpu.make_async_copy(coh_hbm.at[f, pl.ds(0, 2)], coh.at[pl.ds(0, 2)], sems.at[1])
    load_rest = pltpu.make_async_copy(coh_hbm.at[f, pl.ds(2, K - 2)], coh.at[pl.ds(2, K - 2)], sems.at[2])
    load_res.start()
    load_first.start()
    load_rest.start()
    gradient_operands(jall, me, w2, selc, lq, lc, nq, nr)
    load_res.wait()
    load_first.wait()
    gradient(coh, wgt, res, lq, lc, nq, nr, ((y0, a0), (y1, a1)), row, col, groups, load_rest.wait)
    for hop, out in enumerate((col0, col1, col2, col3)):
        out[...] = col[me ^ hop]


def whole(x):
    return pl.BlockSpec(x.shape, lambda i: (0,) * x.ndim)


def spec(shape):
    return pl.BlockSpec(shape, lambda i: (0,) * len(shape))


def call_model(f, me, pieces, factor, coh, vis, flags, sels):
    G = factor.shape[0]
    S = G * LANES
    sc = operand_scratch(G)
    outs = [((G, 8 * K, LANES), None), ((2, 2, 2, ROWS, S), 3), ((ROWS, S), 0), ((8, 128), None)]

    def piece_spec(x):
        at = f if x.shape[0] > 1 else 0
        return pl.BlockSpec((1, *x.shape[1:]), lambda i: (at, 0, 0))

    def out_spec(shape, dim):
        if dim is None:
            return spec(shape)
        block = shape[:dim] + (16,) + shape[dim + 1:]
        return pl.BlockSpec(block, lambda i: tuple(i if d == dim else 0 for d in range(len(shape))))

    return pl.pallas_call(
        model, grid=(TILES,),
        out_shape=[jax.ShapeDtypeStruct(s, F32) for s, _ in outs],
        in_specs=[pl.BlockSpec(memory_space=pltpu.SMEM)] + [piece_spec(x) for x in pieces] + [
            whole(factor),
            pl.BlockSpec((1, K, 2, 16, S), lambda i: (f, 0, 0, i, 0)),
            pl.BlockSpec((1, 2, 2, 2, 16, S), lambda i: (f, 0, 0, 0, i, 0)),
            pl.BlockSpec((1, *flags.shape[1:]), lambda i: (f, 0, 0)),
            whole(sels[0]), whole(sels[1]),
        ],
        out_specs=[out_spec(*o) for o in outs],
        scratch_shapes=[pltpu.VMEM((ROWS, S), F32), *sc["model"]],
        cost_estimate=pl.CostEstimate(flops=8_000_000_000, bytes_accessed=10_000_000, transcendentals=0),
    )(me, *pieces, factor, coh, vis, flags, sels[0], sels[1])


def call_grad(f, me, jall, coh, res, wgt, sels):
    G = jall.shape[0]
    sc = operand_scratch(G)
    outs = [(9 * K, ROWS)] * 5
    return pl.pallas_call(
        functools.partial(grad_kernel, f), grid=(1,),
        out_shape=[jax.ShapeDtypeStruct(s, F32) for s in outs],
        in_specs=[pl.BlockSpec(memory_space=pltpu.SMEM), whole(jall), pl.BlockSpec(memory_space=pl.ANY), pl.BlockSpec(memory_space=pl.ANY),
                  whole(wgt), whole(sels[0]), whole(sels[2])],
        out_specs=[spec(s) for s in outs],
        scratch_shapes=[pltpu.VMEM(coh.shape[1:], BF), pltpu.VMEM(res.shape, F32), pltpu.SemaphoreType.DMA((3,)),
                        pltpu.VMEM((G, 9 * K, ROWS), F32), *sc["grad"], *sc["bufs"]],
        cost_estimate=pl.CostEstimate(flops=20_000_000_000, bytes_accessed=10_000_000, transcendentals=0),
    )(me, jall, coh, res, wgt, sels[0], sels[2])


def beam_factor(beam, group_of):
    groups = beam.shape[0]
    onehot = (group_of[None, :] == jnp.arange(groups, dtype=jnp.int32)[:, None]).astype(F32)
    return jnp.sum(beam[:, :, None] * onehot[:, None, :], axis=0)


def hop_pairs(hop, count):
    return [(i, i ^ hop) for i in range(count)]


def on_device(gains, coherency, vis_data, flags, beam, group_of):
    chan_dev = gains.shape[0]
    row_count = gains.shape[5]
    stn_count = lax.axis_size(STN)
    chan_count = lax.axis_size(CHAN)
    me = lax.axis_index(STN).astype(jnp.int32)
    first_row = me * row_count
    all_channels = chan_dev * chan_count
    all_stations = row_count * stn_count

    raw = gains.reshape(chan_dev, 8 * K, row_count)
    over = [lax.ppermute(raw[f:f + 1], STN, hop_pairs(2, stn_count)) for f in range(chan_dev)]
    mate = lax.ppermute(raw, STN, hop_pairs(1, stn_count))
    far = [lax.ppermute(over[0], STN, hop_pairs(1, stn_count))]
    far.append(lax.ppermute(over[1], STN, hop_pairs(1, stn_count)))
    factor = beam_factor(beam, group_of).reshape(K, stn_count, row_count).swapaxes(0, 1)
    row_factor = lax.dynamic_index_in_dim(factor, me, 0, False)

    up = [(i, i + 1) for i in range(chan_count - 1)]
    down = [(i + 1, i) for i in range(chan_count - 1)]
    before, after = lax.ppermute(gains, CHAN, up), lax.ppermute(gains, CHAN, down)
    extended = jnp.concatenate([before, gains, after], axis=0)
    second = extended[2:] - 2.0 * extended[1:-1] + extended[:-2]
    positions = lax.axis_index(CHAN) * chan_dev - 1 + jnp.arange(chan_dev + 2, dtype=jnp.int32)
    inside = ((positions >= 1) & (positions <= all_channels - 2)).astype(F32)
    second = second * inside[:, None, None, None, None, None]
    smooth_grad = second[:-2] - 2.0 * second[1:-1] + second[2:]
    own_second = second[1:-1]
    smooth_local = jnp.sum(own_second * own_second)

    blocks = jnp.arange(flags.shape[1], dtype=jnp.int32) + first_row // BLK
    selves = blocks[:, None] == jnp.arange(flags.shape[2], dtype=jnp.int32)[None, :]
    local_count = jnp.sum(flags * jnp.where(selves, BLK * (BLK - 1), BLK * BLK)[None]).astype(F32)

    sels = tuple(jnp.asarray(x, BF) for x in selections())
    me1 = me[None]
    jall0, res0, wgt0, sq0 = call_model(0, me1, (raw, mate, over[0], far[0]), factor, coherency, vis_data, flags, sels)
    jall1, res1, wgt1, sq1 = call_model(1, me1, (raw, mate, over[1], far[1]), factor, coherency, vis_data, flags, sels)
    lane = jnp.arange(row_count)
    packed = jnp.where(lane == 0, local_count, jnp.where(lane == 1, jnp.sum(sq0 + sq1), jnp.where(lane == 2, smooth_local, 0.0)))

    arrived = lax.all_to_all(jnp.broadcast_to(packed, (lax.axis_size(NEAR), row_count)), NEAR, 0, 0, tiled=True)
    row0, *cols0 = call_grad(0, me1, jall0, coherency, res0, wgt0, sels)
    partial = jnp.sum(arrived, axis=0)
    arrived = lax.all_to_all(jnp.broadcast_to(partial, (lax.axis_size(OUTER), row_count)), OUTER, 0, 0, tiled=True)
    cols0 = cols0[:1] + [lax.ppermute(cols0[h], STN, hop_pairs(h, stn_count)) for h in range(1, stn_count)]
    row1, *cols1 = call_grad(1, me1, jall1, coherency, res1, wgt1, sels)
    cols1 = cols1[:1] + [lax.ppermute(cols1[h], STN, hop_pairs(h, stn_count)) for h in range(1, stn_count)]
    totals = jnp.sum(arrived, axis=0)

    norm_scale = all_channels * all_stations / totals[0]
    steps = []
    for f, (row, cols) in enumerate(((row0, cols0), (row1, cols1))):
        both = row + (cols[0] + cols[1]) + (cols[2] + cols[3])
        grad = both[:8 * K].reshape(2, 2, 2, K, row_count).swapaxes(0, 1)
        curv = both[8 * K:]
        gradient_f = norm_scale * row_factor * grad + smooth_weight * smooth_grad[f]
        curvature = norm_scale * row_factor * row_factor * curv + damping
        steps.append(gradient_f / curvature)
    gain_step = jnp.stack(steps)
    loss_value = (norm_scale * totals[1] + smooth_weight * totals[2]) / (all_channels * all_stations)
    return gain_step, loss_value


def solution(mesh):
    parts = Mesh(mesh.devices.reshape(4, 2, 8, 4), ("chan_x", "chan_y", "chan_z", "stn"))
    in_specs = (
        P(CHAN, None, None, None, None, STN),
        P(CHAN, None, None, STN, None),
        P(CHAN, None, None, None, STN, None),
        P(CHAN, STN, None),
        P(),
        P(),
    )
    out_specs = (P(CHAN, None, None, None, None, STN), P())

    return jax.shard_map(on_device, mesh=parts, in_specs=in_specs, out_specs=out_specs, check_vma=False)
```

```python
import functools

import jax
import jax.numpy as jnp
import numpy as np
from jax import lax
from jax.experimental import pallas as pl
from jax.experimental.pallas import tpu as pltpu
from jax.sharding import Mesh
from jax.sharding import PartitionSpec as P


BF = jnp.bfloat16
F32 = jnp.float32
CHAN = ("chan_x", "chan_y", "chan_z")
STN = "stn"
OUTER = "chan_z"
INNER = ("chan_x", "chan_y")
smooth_weight = 0.05
damping = 0.3


def selections():
    sel_w = np.zeros((64, 16), np.float32)
    sel_l = np.zeros((2, 16, 16), np.float32)
    for s in range(2):
        for t in range(2):
            for i in range(2):
                for r in range(2):
                    kk = ((s * 2 + t) * 2 + i) * 2 + r
                    for a in range(2):
                        sel_l[a, s * 8 + r * 4 + a * 2 + i, kk] = 1.0
                        sel_w[a * 16 + kk, t * 8 + r * 4 + a * 2 + i] = 1.0
                        sel_w[32 + a * 16 + kk, t * 8 + (1 - r) * 4 + a * 2 + i] = -1.0 if r == 0 else 1.0
    sel_c = np.zeros((2, 16, 16), np.float32)
    sel_q = np.zeros((4, 16, 16), np.float32)
    for s in range(2):
        for a in range(2):
            for i in range(2):
                re, im = s * 8 + a * 2 + i, s * 8 + 4 + a * 2 + i
                sel_c[a, s * 8 + i, re] = -1.0
                sel_c[a, s * 8 + 2 + i, im] = -1.0
                sel_c[a, s * 8 + 4 + i, im] = -1.0
                sel_c[a, s * 8 + 6 + i, re] = 1.0
                for half in range(2):
                    row = s * 8 + half * 4 + i
                    sel_q[a * 2, row, re] = -1.0
                    sel_q[a * 2, row + 2, im] = -1.0
                    sel_q[a * 2 + 1, row, im] = 1.0
                    sel_q[a * 2 + 1, row + 2, re] = -1.0
    w2 = np.concatenate([sel_w, sel_q.reshape(64, 16)], axis=0)
    return w2, sel_l, sel_c.reshape(32, 16)


def operands():
    return tuple(jnp.asarray(x, BF) for x in selections())


def dot(a, b):
    return jnp.dot(a, b, preferred_element_type=F32)


def dot_t(a, b):
    return lax.dot_general(a, b, (((1,), (1,)), ((), ())), preferred_element_type=F32)


def dot_l(a, b):
    return lax.dot_general(a, b, (((0,), (0,)), ((), ())), preferred_element_type=F32)


def split(x):
    high = x.astype(BF)
    return high, (x - high.astype(F32)).astype(BF)


def parts_of(x):
    high = x.astype(BF).astype(F32)
    return jnp.concatenate([high, x - high], axis=0).astype(BF)


K = 16
ROWS = 128
LANES = 128
TILES = ROWS // 16
STEP = 2


def weights_of(first, flags, wgt, groups):
    blocks, cols = flags.shape
    rows8 = lax.broadcasted_iota(jnp.int32, (ROWS, blocks), 0) // 16 == lax.broadcasted_iota(jnp.int32, (ROWS, blocks), 1)
    wide = dot(rows8.astype(F32).astype(BF), flags.astype(F32).astype(BF)).astype(BF)
    for g in range(groups):
        at = (lax.broadcasted_iota(jnp.int32, (cols, LANES), 1) + g * LANES) // 16
        at = at == lax.broadcasted_iota(jnp.int32, (cols, LANES), 0)
        full = dot(wide, at.astype(F32).astype(BF))
        row_id = lax.broadcasted_iota(jnp.int32, (ROWS, LANES), 0) + first
        col_id = lax.broadcasted_iota(jnp.int32, (ROWS, LANES), 1) + g * LANES
        wgt[:, g * LANES:(g + 1) * LANES] = jnp.where(row_id == col_id, 0.0, full)


def in_fours(turn):
    def four(i, _):
        for n in range(4):
            turn(i * 4 + n)
        return 0

    lax.fori_loop(0, K // 4, four, 0)


def model_operands(jall, me, w2, sell, wr, wi, lr):
    groups = jall.shape[0]

    def turn(k):
        for g in range(groups):
            w = dot(w2[0:64], parts_of(jall[g, pl.ds(k, 8, stride=16), :])).astype(BF)
            for b in range(2):
                wr[k, g, :, b * 128:(b + 1) * 128] = w[b * 16:(b + 1) * 16]
                wi[k, g, :, b * 128:(b + 1) * 128] = w[32 + b * 16:48 + b * 16]
        hm = parts_of(jall[me, pl.ds(k, 8, stride=16), :])
        for a in range(2):
            l = dot_l(hm, sell[a]).astype(BF)
            for t in range(TILES):
                lr[k, t, a * 16:(a + 1) * 16, :] = l[t * 16:(t + 1) * 16]

    in_fours(turn)


def model(me_ref, own, mate, over, far, factor, coh, vis, flags, w2, sell, smooth, earlier, jall, res, wgt, stats, w_all, wr, wi, lr):
    groups = jall.shape[0]
    t = pl.program_id(0)
    me = me_ref[0]

    @pl.when(t == 0)
    def _():
        for hop, piece in enumerate((own, mate, over, far)):
            g = me ^ hop
            scale = factor[g]
            for plane in range(8):
                at = slice(plane * K, (plane + 1) * K)
                jall[g, at, :] = piece[0, at, :] * scale
        weights_of(me * ROWS, flags[0], w_all, groups)
        model_operands(jall, me, w2, sell, wr, wi, lr)
        stats[...] = earlier[...]
        stats[16:32] += smooth[...]

    def tile(n, _):
        rows = pl.ds(pl.multiple_of(n * 16, 16), 16)
        at = t * STEP + n
        w_rows = w_all[pl.ds(pl.multiple_of(at * 16, 16), 16), :]
        wgt[rows, :] = w_rows
        total = jnp.zeros((16, 128), F32)
        used = jnp.zeros((16, 128), F32)
        for g in range(groups):
            cols = slice(g * 128, (g + 1) * 128)
            acc = [[[jnp.zeros((16, 128), F32)] * 2 for _ in range(2)] for _ in range(2)]
            for k in range(K):
                o_re = dot(lr[k, at], wr[k, g])
                o_im = dot(lr[k, at], wi[k, g])
                c_re = coh[0, k, 0, rows, cols].astype(F32)
                c_im = coh[0, k, 1, rows, cols].astype(F32)
                for a in range(2):
                    for b in range(2):
                        re = o_re[a * 16:(a + 1) * 16, b * 128:(b + 1) * 128]
                        im = o_im[a * 16:(a + 1) * 16, b * 128:(b + 1) * 128]
                        acc[a][b] = [acc[a][b][0] + c_re * re - c_im * im,
                                     acc[a][b][1] + c_re * im + c_im * re]
            w = w_rows[:, cols]
            used = used + w
            for a in range(2):
                for b in range(2):
                    for r in range(2):
                        v = w * (vis[0, r, a, b, rows, cols].astype(F32) - acc[a][b][r])
                        res[b, r, a, rows, cols] = v
                        total = total + v * v
        stats[0:8] += total[:8] + total[8:]
        stats[8:16] += used[:8] + used[8:]
        return 0

    lax.fori_loop(0, STEP, tile, 0)


def norms(x):
    return parts_of(jnp.broadcast_to(jnp.sum(x * x, axis=0, keepdims=True), (8, LANES)))


def gradient_operands(jall, me, w2, selc, lq, lc, nq, nr):
    groups = jall.shape[0]
    span = groups * LANES

    def turn(k):
        for g in range(groups):
            x = jall[g, pl.ds(k, 8, stride=16), :]
            w = dot(w2[64:128], parts_of(x)).astype(BF)
            for j in range(4):
                lq[k, :, j * span + g * 128:j * span + (g + 1) * 128] = w[j * 16:j * 16 + 16]
            nq[k, :, g * 128:(g + 1) * 128] = norms(x)
        x = jall[me, pl.ds(k, 8, stride=16), :]
        c = dot(selc[...], parts_of(x)).astype(BF)
        for a in range(2):
            lc[k, :, a * 128:(a + 1) * 128] = c[a * 16:(a + 1) * 16]
        nr[k] = norms(x)

    in_fours(turn)


def gradient(coh, wgt, res, lq, lc, nq, nr, bufs, row, col, groups, rest):
    span = groups * LANES
    halves = groups // 2

    def fill(k, t, h, y, am):
        cols = slice(h * 256, (h + 1) * 256)
        rows = slice(t * 16, (t + 1) * 16)
        c_re = coh[k, 0, rows, cols].astype(F32)
        c_im = coh[k, 1, rows, cols].astype(F32)
        for a in range(2):
            at = slice(a * ROWS + t * 16, a * ROWS + t * 16 + 16)
            for b in range(2):
                r_re = res[b, 0, a, rows, cols]
                r_im = res[b, 1, a, rows, cols]
                for r, v in ((0, c_re * r_re + c_im * r_im), (1, c_re * r_im - c_im * r_re)):
                    high, low = split(v)
                    y[b * 2 + r, h, 0, at, :] = high
                    y[b * 2 + r, h, 1, at, :] = low
        high, low = split(wgt[rows, cols] * (c_re * c_re + c_im * c_im))
        am[h, rows, :] = high
        am[h, ROWS + t * 16:ROWS + t * 16 + 16, :] = low

    top = lax.broadcasted_iota(jnp.int32, (8, 128), 0) < 4

    def reduce_part(k, j, h, s, y, cell):
        tile = y[j, h, s]
        c = dot(lc[k], tile)
        r = dot_t(lq[k, :, j * span + h * 256:j * span + (h + 1) * 256], tile)
        c = c[:8] + c[8:]
        cell[0][j, h] = c if s == 0 else cell[0][j, h] + c
        cell[1] = r if cell[1] is None else cell[1] + r

    def reduce_end(k, am, cell):
        r = cell[1][:8] + cell[1][8:]
        row[pl.ds(k, 8, stride=16), :] = jnp.where(top, r[:, :ROWS], r[:, ROWS:])
        for g in range(groups):
            h, cols = g // 2, slice(g % 2 * 128, g % 2 * 128 + 128)
            c = [cell[0][j, h][:, cols] for j in range(4)]
            t0 = c[0] + pltpu.roll(c[1], 4, 0)
            t1 = pltpu.roll(c[2], 4, 0) + c[3]
            col[g, pl.ds(k, 8, stride=16), :] = jnp.where(top, t0, t1)
        total = None
        n_row = jnp.concatenate([nr[k], nr[k]], axis=1)
        for h in range(halves):
            tile = am[h]
            cc = dot(n_row, tile)
            cc = cc[0:1] + cc[8:9]
            for g in range(2):
                col[h * 2 + g, pl.ds(128 + k, 1), :] = cc[:, g * 128:(g + 1) * 128]
            cr = dot_t(nq[k, :, h * 256:(h + 1) * 256], tile)
            cr = cr[0:1] + cr[8:9]
            cr = cr[:, :ROWS] + cr[:, ROWS:]
            total = cr if total is None else total + cr
        row[pl.ds(128 + k, 1), :] = total

    fills = [(t, h) for t in range(TILES) for h in range(halves)]
    dots = [(j, h, s) for j in range(4) for h in range(halves) for s in range(2)]
    (y0, a0), (y1, a1) = bufs
    for t, h in fills:
        fill(0, t, h, y0, a0)
    rest()

    def pair(i, _):
        for step, (y, am, y_next, am_next) in enumerate(((y0, a0, y1, a1), (y1, a1, y0, a0))):
            k = 2 * i + step
            k_next = jnp.minimum(k + 1, K - 1)
            cell = [{}, None]
            for (t, h), part in zip(fills, dots):
                reduce_part(k, *part, y, cell)
                fill(k_next, t, h, y_next, am_next)
            reduce_end(k, am, cell)
        return 0

    lax.fori_loop(0, K // 2, pair, 0)


def operand_scratch(G):
    S = G * 128
    return dict(
        model=[pltpu.VMEM((K, G, 16, 256), BF), pltpu.VMEM((K, G, 16, 256), BF), pltpu.VMEM((K, TILES, 32, 16), BF)],
        grad=[pltpu.VMEM((K, 16, 4 * S), BF), pltpu.VMEM((K, 16, 2 * ROWS), BF), pltpu.VMEM((K, 16, S), BF), pltpu.VMEM((K, 16, ROWS), BF)],
        bufs=[pltpu.VMEM((4, G // 2, 2, 2 * ROWS, 256), BF), pltpu.VMEM((G // 2, 2 * ROWS, 256), BF)] * 2,
    )


def grad_kernel(f, me_ref, jall, coh_hbm, res_hbm, wgt, w2, selc, row, col0, col1, col2, col3,
                coh, res, sems, col, lq, lc, nq, nr, y0, a0, y1, a1):
    groups = jall.shape[0]
    me = me_ref[0]
    load_res = pltpu.make_async_copy(res_hbm, res, sems.at[0])
    load_first = pltpu.make_async_copy(coh_hbm.at[f, pl.ds(0, 2)], coh.at[pl.ds(0, 2)], sems.at[1])
    load_rest = pltpu.make_async_copy(coh_hbm.at[f, pl.ds(2, K - 2)], coh.at[pl.ds(2, K - 2)], sems.at[2])
    load_res.start()
    load_first.start()
    load_rest.start()
    gradient_operands(jall, me, w2, selc, lq, lc, nq, nr)
    load_res.wait()
    load_first.wait()
    gradient(coh, wgt, res, lq, lc, nq, nr, ((y0, a0), (y1, a1)), row, col, groups, load_rest.wait)
    for hop, out in enumerate((col0, col1, col2, col3)):
        out[...] = col[me ^ hop]


def whole(x):
    return pl.BlockSpec(x.shape, lambda i: (0,) * x.ndim)


def spec(shape):
    return pl.BlockSpec(shape, lambda i: (0,) * len(shape))


def call_model(f, me, pieces, factor, coh, vis, flags, sels, smooth, earlier):
    G = factor.shape[0]
    S = G * LANES
    sc = operand_scratch(G)
    outs = [((G, 8 * K, LANES), None), ((2, 2, 2, ROWS, S), 3), ((ROWS, S), 0), ((32, LANES), None)]

    if earlier is None:
        earlier, smooth = jnp.zeros((32, LANES), F32), jnp.zeros((16, LANES), F32)

    def piece_spec(x):
        at = f if x.shape[0] > 1 else 0
        return pl.BlockSpec((1, *x.shape[1:]), lambda i: (at, 0, 0))

    def out_spec(shape, dim):
        if dim is None:
            return spec(shape)
        block = shape[:dim] + (16 * STEP,) + shape[dim + 1:]
        return pl.BlockSpec(block, lambda i: tuple(i if d == dim else 0 for d in range(len(shape))))

    return pl.pallas_call(
        model, grid=(TILES // STEP,),
        out_shape=[jax.ShapeDtypeStruct(s, F32) for s, _ in outs],
        in_specs=[pl.BlockSpec(memory_space=pltpu.SMEM)] + [piece_spec(x) for x in pieces] + [
            whole(factor),
            pl.BlockSpec((1, K, 2, 16 * STEP, S), lambda i: (f, 0, 0, i, 0)),
            pl.BlockSpec((1, 2, 2, 2, 16 * STEP, S), lambda i: (f, 0, 0, 0, i, 0)),
            pl.BlockSpec((1, *flags.shape[1:]), lambda i: (f, 0, 0)),
            whole(sels[0]), whole(sels[1]), whole(smooth), whole(earlier),
        ],
        out_specs=[out_spec(*o) for o in outs],
        scratch_shapes=[pltpu.VMEM((ROWS, S), F32), *sc["model"]],
        cost_estimate=pl.CostEstimate(flops=8_000_000_000, bytes_accessed=10_000_000, transcendentals=0),
        compiler_params=pltpu.CompilerParams(vmem_limit_bytes=24 << 20),
    )(me, *pieces, factor, coh, vis, flags, sels[0], sels[1], smooth, earlier)


def call_grad(f, me, jall, coh, res, wgt, sels):
    G = jall.shape[0]
    sc = operand_scratch(G)
    outs = [(9 * K, ROWS)] * 5
    return pl.pallas_call(
        functools.partial(grad_kernel, f), grid=(1,),
        out_shape=[jax.ShapeDtypeStruct(s, F32) for s in outs],
        in_specs=[pl.BlockSpec(memory_space=pltpu.SMEM), whole(jall), pl.BlockSpec(memory_space=pl.ANY), pl.BlockSpec(memory_space=pl.ANY),
                  whole(wgt), whole(sels[0]), whole(sels[2])],
        out_specs=[spec(s) for s in outs],
        scratch_shapes=[pltpu.VMEM(coh.shape[1:], BF), pltpu.VMEM(res.shape, F32), pltpu.SemaphoreType.DMA((3,)),
                        pltpu.VMEM((G, 9 * K, ROWS), F32), *sc["grad"], *sc["bufs"]],
        cost_estimate=pl.CostEstimate(flops=20_000_000_000, bytes_accessed=10_000_000, transcendentals=0),
        compiler_params=pltpu.CompilerParams(vmem_limit_bytes=36 << 20),
    )(me, jall, coh, res, wgt, sels[0], sels[2])


def beam_factor(beam, group_of):
    groups = beam.shape[0]
    onehot = (group_of[None, :] == jnp.arange(groups, dtype=jnp.int32)[:, None]).astype(F32)
    return jnp.sum(beam[:, :, None] * onehot[:, None, :], axis=0)


def hop_pairs(hop, count):
    return [(i, i ^ hop) for i in range(count)]


def summed(values, axes):
    count = lax.axis_size(axes)
    parts = [values] + [lax.ppermute(values, axes, hop_pairs(hop, count)) for hop in range(1, count)]
    while len(parts) > 1:
        parts = [parts[i] + parts[i + 1] for i in range(0, len(parts), 2)]
    return parts[0]


def on_device(gains, coherency, vis_data, flags, beam, group_of):
    chan_dev = gains.shape[0]
    row_count = gains.shape[5]
    stn_count = lax.axis_size(STN)
    chan_count = lax.axis_size(CHAN)
    me = lax.axis_index(STN).astype(jnp.int32)
    all_channels = chan_dev * chan_count
    all_stations = row_count * stn_count

    raw = gains.reshape(chan_dev, 8 * K, row_count)
    over = [lax.ppermute(raw[f:f + 1], STN, hop_pairs(2, stn_count)) for f in range(chan_dev)]
    mate = lax.ppermute(raw, STN, hop_pairs(1, stn_count))
    far = [lax.ppermute(over[0], STN, hop_pairs(1, stn_count))]
    far.append(lax.ppermute(over[1], STN, hop_pairs(1, stn_count)))
    factor = beam_factor(beam, group_of).reshape(K, stn_count, row_count).swapaxes(0, 1)
    row_factor = lax.dynamic_index_in_dim(factor, me, 0, False)

    up = [(i, i + 1) for i in range(chan_count - 1)]
    down = [(i + 1, i) for i in range(chan_count - 1)]
    before, after = lax.ppermute(gains, CHAN, up), lax.ppermute(gains, CHAN, down)
    extended = jnp.concatenate([before, gains, after], axis=0)
    second = extended[2:] - 2.0 * extended[1:-1] + extended[:-2]
    positions = lax.axis_index(CHAN) * chan_dev - 1 + jnp.arange(chan_dev + 2, dtype=jnp.int32)
    inside = ((positions >= 1) & (positions <= all_channels - 2)).astype(F32)
    second = second * inside[:, None, None, None, None, None]
    smooth_grad = second[:-2] - 2.0 * second[1:-1] + second[2:]
    own_second = second[1:-1]
    smooth_local = jnp.sum(own_second * own_second, axis=(0, 1, 2, 3))

    sels = operands()
    me1 = me[None]
    jall0, res0, wgt0, stats = call_model(0, me1, (raw, mate, over[0], far[0]), factor, coherency, vis_data, flags, sels, None, None)
    jall1, res1, wgt1, stats = call_model(1, me1, (raw, mate, over[1], far[1]), factor, coherency, vis_data, flags, sels, smooth_local, stats)

    stats = summed(stats, OUTER)
    row0, *cols0 = call_grad(0, me1, jall0, coherency, res0, wgt0, sels)
    stats = summed(stats, INNER)
    cols0 = cols0[:1] + [lax.ppermute(cols0[h], STN, hop_pairs(h, stn_count)) for h in range(1, stn_count)]
    row1, *cols1 = call_grad(1, me1, jall1, coherency, res1, wgt1, sels)
    cols1 = cols1[:1] + [lax.ppermute(cols1[h], STN, hop_pairs(h, stn_count)) for h in range(1, stn_count)]
    stats = summed(stats, STN)
    sq, count, smooth = jnp.sum(stats[:8]), jnp.sum(stats[8:16]), jnp.sum(stats[16:])

    norm_scale = all_channels * all_stations / count
    steps = []
    for f, (row, cols) in enumerate(((row0, cols0), (row1, cols1))):
        both = row + (cols[0] + cols[1]) + (cols[2] + cols[3])
        grad = both[:8 * K].reshape(2, 2, 2, K, row_count).swapaxes(0, 1)
        curv = both[8 * K:]
        gradient_f = norm_scale * row_factor * grad + smooth_weight * smooth_grad[f]
        curvature = norm_scale * row_factor * row_factor * curv + damping
        steps.append(gradient_f / curvature)
    gain_step = jnp.stack(steps)
    loss_value = (norm_scale * sq + smooth_weight * smooth) / (all_channels * all_stations)
    return gain_step, loss_value


def solution(mesh):
    parts = Mesh(mesh.devices.reshape(4, 2, 8, 4), ("chan_x", "chan_y", "chan_z", "stn"))
    in_specs = (
        P(CHAN, None, None, None, None, STN),
        P(CHAN, None, None, STN, None),
        P(CHAN, None, None, None, STN, None),
        P(CHAN, STN, None),
        P(),
        P(),
    )
    out_specs = (P(CHAN, None, None, None, None, STN), P())

    return jax.shard_map(on_device, mesh=parts, in_specs=in_specs, out_specs=out_specs, check_vma=False)
```

```python
import functools

import jax
import jax.numpy as jnp
import numpy as np
from jax import lax
from jax.experimental import pallas as pl
from jax.experimental.pallas import tpu as pltpu
from jax.sharding import Mesh
from jax.sharding import PartitionSpec as P


BF = jnp.bfloat16
F32 = jnp.float32
CHAN = ("chan_x", "chan_y", "chan_z")
STN = "stn"
ALL = ("chan_x", "chan_y", "chan_z", "stn")
smooth_weight = 0.05
damping = 0.3


def selections():
    sel_w = np.zeros((64, 16), np.float32)
    sel_l = np.zeros((2, 16, 16), np.float32)
    for s in range(2):
        for t in range(2):
            for i in range(2):
                for r in range(2):
                    kk = ((s * 2 + t) * 2 + i) * 2 + r
                    for a in range(2):
                        sel_l[a, s * 8 + r * 4 + a * 2 + i, kk] = 1.0
                        sel_w[a * 16 + kk, t * 8 + r * 4 + a * 2 + i] = 1.0
                        sel_w[32 + a * 16 + kk, t * 8 + (1 - r) * 4 + a * 2 + i] = -1.0 if r == 0 else 1.0
    sel_c = np.zeros((2, 16, 16), np.float32)
    sel_q = np.zeros((4, 16, 16), np.float32)
    for s in range(2):
        for a in range(2):
            for i in range(2):
                re, im = s * 8 + a * 2 + i, s * 8 + 4 + a * 2 + i
                sel_c[a, s * 8 + i, re] = -1.0
                sel_c[a, s * 8 + 2 + i, im] = -1.0
                sel_c[a, s * 8 + 4 + i, im] = -1.0
                sel_c[a, s * 8 + 6 + i, re] = 1.0
                for half in range(2):
                    row = s * 8 + half * 4 + i
                    sel_q[a * 2, row, re] = -1.0
                    sel_q[a * 2, row + 2, im] = -1.0
                    sel_q[a * 2 + 1, row, im] = 1.0
                    sel_q[a * 2 + 1, row + 2, re] = -1.0
    w2 = np.concatenate([sel_w, sel_q.reshape(64, 16)], axis=0)
    return w2, sel_l, sel_c.reshape(32, 16)


def operands():
    return tuple(jnp.asarray(x, BF) for x in selections())


def dot(a, b):
    return jnp.dot(a, b, preferred_element_type=F32)


def dot_t(a, b):
    return lax.dot_general(a, b, (((1,), (1,)), ((), ())), preferred_element_type=F32)


def dot_l(a, b):
    return lax.dot_general(a, b, (((0,), (0,)), ((), ())), preferred_element_type=F32)


def split(x):
    high = x.astype(BF)
    return high, (x - high.astype(F32)).astype(BF)


def parts_of(x):
    high = x.astype(BF).astype(F32)
    return jnp.concatenate([high, x - high], axis=0).astype(BF)


K = 16
ROWS = 128
LANES = 128
TILES = ROWS // 16
STEP = 2


def weights_of(first, flags, wgt, groups):
    blocks, cols = flags.shape
    rows8 = lax.broadcasted_iota(jnp.int32, (ROWS, blocks), 0) // 16 == lax.broadcasted_iota(jnp.int32, (ROWS, blocks), 1)
    wide = dot(rows8.astype(F32).astype(BF), flags.astype(F32).astype(BF)).astype(BF)
    for g in range(groups):
        at = (lax.broadcasted_iota(jnp.int32, (cols, LANES), 1) + g * LANES) // 16
        at = at == lax.broadcasted_iota(jnp.int32, (cols, LANES), 0)
        full = dot(wide, at.astype(F32).astype(BF))
        row_id = lax.broadcasted_iota(jnp.int32, (ROWS, LANES), 0) + first
        col_id = lax.broadcasted_iota(jnp.int32, (ROWS, LANES), 1) + g * LANES
        wgt[:, g * LANES:(g + 1) * LANES] = jnp.where(row_id == col_id, 0.0, full)


def in_fours(turn):
    def four(i, _):
        for n in range(4):
            turn(i * 4 + n)
        return 0

    lax.fori_loop(0, K // 4, four, 0)


def model_operands(jall, me, w2, sell, wr, wi, lr):
    groups = jall.shape[0]

    def turn(k):
        for g in range(groups):
            w = dot(w2[0:64], parts_of(jall[g, pl.ds(k, 8, stride=16), :])).astype(BF)
            for b in range(2):
                wr[k, g, :, b * 128:(b + 1) * 128] = w[b * 16:(b + 1) * 16]
                wi[k, g, :, b * 128:(b + 1) * 128] = w[32 + b * 16:48 + b * 16]
        hm = parts_of(jall[me, pl.ds(k, 8, stride=16), :])
        for a in range(2):
            l = dot_l(hm, sell[a]).astype(BF)
            for t in range(TILES):
                lr[k, t, a * 16:(a + 1) * 16, :] = l[t * 16:(t + 1) * 16]

    in_fours(turn)


def model(me_ref, own, mate, over, far, factor, coh, vis, flags, w2, sell, smooth, earlier, jall, res, wgt, stats, *rest):
    *spread, w_all, wr, wi, lr = rest
    spread = spread[0] if spread else None
    groups = jall.shape[0]
    t = pl.program_id(0)
    me = me_ref[0]

    @pl.when(t == 0)
    def _():
        for hop, piece in enumerate((own, mate, over, far)):
            g = me ^ hop
            scale = factor[g]
            for plane in range(8):
                at = slice(plane * K, (plane + 1) * K)
                jall[g, at, :] = piece[0, at, :] * scale
        weights_of(me * ROWS, flags[0], w_all, groups)
        model_operands(jall, me, w2, sell, wr, wi, lr)
        stats[...] = earlier[...]
        stats[16:32] += smooth[...]

    def tile(n, _):
        rows = pl.ds(pl.multiple_of(n * 16, 16), 16)
        at = t * STEP + n
        w_rows = w_all[pl.ds(pl.multiple_of(at * 16, 16), 16), :]
        wgt[rows, :] = w_rows
        total = jnp.zeros((16, 128), F32)
        used = jnp.zeros((16, 128), F32)
        for g in range(groups):
            cols = slice(g * 128, (g + 1) * 128)
            acc = [[[jnp.zeros((16, 128), F32)] * 2 for _ in range(2)] for _ in range(2)]
            for k in range(K):
                o_re = dot(lr[k, at], wr[k, g])
                o_im = dot(lr[k, at], wi[k, g])
                c_re = coh[0, k, 0, rows, cols].astype(F32)
                c_im = coh[0, k, 1, rows, cols].astype(F32)
                for a in range(2):
                    for b in range(2):
                        re = o_re[a * 16:(a + 1) * 16, b * 128:(b + 1) * 128]
                        im = o_im[a * 16:(a + 1) * 16, b * 128:(b + 1) * 128]
                        acc[a][b] = [acc[a][b][0] + c_re * re - c_im * im,
                                     acc[a][b][1] + c_re * im + c_im * re]
            w = w_rows[:, cols]
            used = used + w
            for a in range(2):
                for b in range(2):
                    for r in range(2):
                        v = w * (vis[0, r, a, b, rows, cols].astype(F32) - acc[a][b][r])
                        res[b, r, a, rows, cols] = v
                        total = total + v * v
        stats[0:8] += total[:8] + total[8:]
        stats[8:16] += used[:8] + used[8:]
        return 0

    lax.fori_loop(0, STEP, tile, 0)
    if spread is not None:
        @pl.when(t == pl.num_programs(0) - 1)
        def _():
            lane = lax.broadcasted_iota(jnp.int32, spread.shape, 1)
            sums = [jnp.sum(stats[lo:hi]) for lo, hi in ((0, 8), (8, 16), (16, 32))]
            spread[...] = jnp.where(lane == 0, sums[0], jnp.where(lane == 1, sums[1], jnp.where(lane == 2, sums[2], 0.0)))


def norms(x):
    return parts_of(jnp.broadcast_to(jnp.sum(x * x, axis=0, keepdims=True), (8, LANES)))


def gradient_operands(jall, me, w2, selc, lq, lc, nq, nr):
    groups = jall.shape[0]
    span = groups * LANES

    def turn(k):
        for g in range(groups):
            x = jall[g, pl.ds(k, 8, stride=16), :]
            w = dot(w2[64:128], parts_of(x)).astype(BF)
            for j in range(4):
                lq[k, :, j * span + g * 128:j * span + (g + 1) * 128] = w[j * 16:j * 16 + 16]
            nq[k, :, g * 128:(g + 1) * 128] = norms(x)
        x = jall[me, pl.ds(k, 8, stride=16), :]
        c = dot(selc[...], parts_of(x)).astype(BF)
        for a in range(2):
            lc[k, :, a * 128:(a + 1) * 128] = c[a * 16:(a + 1) * 16]
        nr[k] = norms(x)

    in_fours(turn)


def gradient(coh, wgt, res, lq, lc, nq, nr, bufs, row, col, groups, rest):
    span = groups * LANES
    halves = groups // 2

    def fill(k, t, h, y, am):
        cols = slice(h * 256, (h + 1) * 256)
        rows = slice(t * 16, (t + 1) * 16)
        c_re = coh[k, 0, rows, cols].astype(F32)
        c_im = coh[k, 1, rows, cols].astype(F32)
        for a in range(2):
            at = slice(a * ROWS + t * 16, a * ROWS + t * 16 + 16)
            for b in range(2):
                r_re = res[b, 0, a, rows, cols]
                r_im = res[b, 1, a, rows, cols]
                for r, v in ((0, c_re * r_re + c_im * r_im), (1, c_re * r_im - c_im * r_re)):
                    high, low = split(v)
                    y[b * 2 + r, h, 0, at, :] = high
                    y[b * 2 + r, h, 1, at, :] = low
        high, low = split(wgt[rows, cols] * (c_re * c_re + c_im * c_im))
        am[h, rows, :] = high
        am[h, ROWS + t * 16:ROWS + t * 16 + 16, :] = low

    top = lax.broadcasted_iota(jnp.int32, (8, 128), 0) < 4

    def reduce_part(k, j, h, s, y, cell):
        tile = y[j, h, s]
        c = dot(lc[k], tile)
        r = dot_t(lq[k, :, j * span + h * 256:j * span + (h + 1) * 256], tile)
        c = c[:8] + c[8:]
        cell[0][j, h] = c if s == 0 else cell[0][j, h] + c
        cell[1] = r if cell[1] is None else cell[1] + r

    def reduce_end(k, am, cell):
        r = cell[1][:8] + cell[1][8:]
        row[pl.ds(k, 8, stride=16), :] = jnp.where(top, r[:, :ROWS], r[:, ROWS:])
        for g in range(groups):
            h, cols = g // 2, slice(g % 2 * 128, g % 2 * 128 + 128)
            c = [cell[0][j, h][:, cols] for j in range(4)]
            t0 = c[0] + pltpu.roll(c[1], 4, 0)
            t1 = pltpu.roll(c[2], 4, 0) + c[3]
            col[g, pl.ds(k, 8, stride=16), :] = jnp.where(top, t0, t1)
        total = None
        n_row = jnp.concatenate([nr[k], nr[k]], axis=1)
        for h in range(halves):
            tile = am[h]
            cc = dot(n_row, tile)
            cc = cc[0:1] + cc[8:9]
            for g in range(2):
                col[h * 2 + g, pl.ds(128 + k, 1), :] = cc[:, g * 128:(g + 1) * 128]
            cr = dot_t(nq[k, :, h * 256:(h + 1) * 256], tile)
            cr = cr[0:1] + cr[8:9]
            cr = cr[:, :ROWS] + cr[:, ROWS:]
            total = cr if total is None else total + cr
        row[pl.ds(128 + k, 1), :] = total

    fills = [(t, h) for t in range(TILES) for h in range(halves)]
    dots = [(j, h, s) for j in range(4) for h in range(halves) for s in range(2)]
    (y0, a0), (y1, a1) = bufs
    for t, h in fills:
        fill(0, t, h, y0, a0)
    rest()

    def pair(i, _):
        for step, (y, am, y_next, am_next) in enumerate(((y0, a0, y1, a1), (y1, a1, y0, a0))):
            k = 2 * i + step
            k_next = jnp.minimum(k + 1, K - 1)
            cell = [{}, None]
            for (t, h), part in zip(fills, dots):
                reduce_part(k, *part, y, cell)
                fill(k_next, t, h, y_next, am_next)
            reduce_end(k, am, cell)
        return 0

    lax.fori_loop(0, K // 2, pair, 0)


def operand_scratch(G):
    S = G * 128
    return dict(
        model=[pltpu.VMEM((K, G, 16, 256), BF), pltpu.VMEM((K, G, 16, 256), BF), pltpu.VMEM((K, TILES, 32, 16), BF)],
        grad=[pltpu.VMEM((K, 16, 4 * S), BF), pltpu.VMEM((K, 16, 2 * ROWS), BF), pltpu.VMEM((K, 16, S), BF), pltpu.VMEM((K, 16, ROWS), BF)],
        bufs=[pltpu.VMEM((4, G // 2, 2, 2 * ROWS, 256), BF), pltpu.VMEM((G // 2, 2 * ROWS, 256), BF)] * 2,
    )


def grad_kernel(f, me_ref, jall, coh_hbm, res_hbm, wgt, w2, selc, row, col0, col1, col2, col3,
                coh, res, sems, col, lq, lc, nq, nr, y0, a0, y1, a1):
    groups = jall.shape[0]
    me = me_ref[0]
    load_res = pltpu.make_async_copy(res_hbm, res, sems.at[0])
    load_first = pltpu.make_async_copy(coh_hbm.at[f, pl.ds(0, 2)], coh.at[pl.ds(0, 2)], sems.at[1])
    load_rest = pltpu.make_async_copy(coh_hbm.at[f, pl.ds(2, K - 2)], coh.at[pl.ds(2, K - 2)], sems.at[2])
    load_res.start()
    load_first.start()
    load_rest.start()
    gradient_operands(jall, me, w2, selc, lq, lc, nq, nr)
    load_res.wait()
    load_first.wait()
    gradient(coh, wgt, res, lq, lc, nq, nr, ((y0, a0), (y1, a1)), row, col, groups, load_rest.wait)
    for hop, out in enumerate((col0, col1, col2, col3)):
        out[...] = col[me ^ hop]


def whole(x):
    return pl.BlockSpec(x.shape, lambda i: (0,) * x.ndim)


def spec(shape):
    return pl.BlockSpec(shape, lambda i: (0,) * len(shape))


def call_model(f, me, pieces, factor, coh, vis, flags, sels, smooth, earlier, devices=0):
    G = factor.shape[0]
    S = G * LANES
    sc = operand_scratch(G)
    outs = [((G, 8 * K, LANES), None), ((2, 2, 2, ROWS, S), 3), ((ROWS, S), 0), ((32, LANES), None)]
    if devices:
        outs.append(((devices, LANES), None))

    if earlier is None:
        earlier, smooth = jnp.zeros((32, LANES), F32), jnp.zeros((16, LANES), F32)

    operands_in = (coh, vis, flags, sels[0], sels[1])
    if f == 0:
        operands_in = tuple(pltpu.with_memory_space_constraint(x, pltpu.HBM) for x in operands_in)
        pieces = (pltpu.with_memory_space_constraint(pieces[0], pltpu.HBM), *pieces[1:])

    def piece_spec(x):
        at = f if x.shape[0] > 1 else 0
        return pl.BlockSpec((1, *x.shape[1:]), lambda i: (at, 0, 0))

    def out_spec(shape, dim):
        if dim is None:
            return spec(shape)
        block = shape[:dim] + (16 * STEP,) + shape[dim + 1:]
        return pl.BlockSpec(block, lambda i: tuple(i if d == dim else 0 for d in range(len(shape))))

    return pl.pallas_call(
        model, grid=(TILES // STEP,),
        out_shape=[jax.ShapeDtypeStruct(s, F32) for s, _ in outs],
        in_specs=[pl.BlockSpec(memory_space=pltpu.SMEM)] + [piece_spec(x) for x in pieces] + [
            whole(factor),
            pl.BlockSpec((1, K, 2, 16 * STEP, S), lambda i: (f, 0, 0, i, 0)),
            pl.BlockSpec((1, 2, 2, 2, 16 * STEP, S), lambda i: (f, 0, 0, 0, i, 0)),
            pl.BlockSpec((1, *flags.shape[1:]), lambda i: (f, 0, 0)),
            whole(sels[0]), whole(sels[1]), whole(smooth), whole(earlier),
        ],
        out_specs=[out_spec(*o) for o in outs],
        scratch_shapes=[pltpu.VMEM((ROWS, S), F32), *sc["model"]],
        cost_estimate=pl.CostEstimate(flops=8_000_000_000, bytes_accessed=10_000_000, transcendentals=0),
        compiler_params=pltpu.CompilerParams(vmem_limit_bytes=24 << 20),
    )(me, *pieces, factor, *operands_in, smooth, earlier)


def call_grad(f, me, jall, coh, res, wgt, sels):
    G = jall.shape[0]
    sc = operand_scratch(G)
    outs = [(9 * K, ROWS)] * 5
    return pl.pallas_call(
        functools.partial(grad_kernel, f), grid=(1,),
        out_shape=[jax.ShapeDtypeStruct(s, F32) for s in outs],
        in_specs=[pl.BlockSpec(memory_space=pltpu.SMEM), whole(jall), pl.BlockSpec(memory_space=pl.ANY), pl.BlockSpec(memory_space=pl.ANY),
                  whole(wgt), whole(sels[0]), whole(sels[2])],
        out_specs=[spec(s) for s in outs],
        scratch_shapes=[pltpu.VMEM(coh.shape[1:], BF), pltpu.VMEM(res.shape, F32), pltpu.SemaphoreType.DMA((3,)),
                        pltpu.VMEM((G, 9 * K, ROWS), F32), *sc["grad"], *sc["bufs"]],
        cost_estimate=pl.CostEstimate(flops=20_000_000_000, bytes_accessed=10_000_000, transcendentals=0),
        compiler_params=pltpu.CompilerParams(vmem_limit_bytes=36 << 20),
    )(me, jall, pltpu.with_memory_space_constraint(coh, pltpu.HBM), res, wgt, sels[0], sels[2])


def beam_factor(beam, group_of):
    groups = beam.shape[0]
    onehot = (group_of[None, :] == jnp.arange(groups, dtype=jnp.int32)[:, None]).astype(F32)
    return jnp.sum(beam[:, :, None] * onehot[:, None, :], axis=0)


def hop_pairs(hop, count):
    return [(i, i ^ hop) for i in range(count)]


def on_device(gains, coherency, vis_data, flags, beam, group_of):
    chan_dev = gains.shape[0]
    row_count = gains.shape[5]
    stn_count = lax.axis_size(STN)
    chan_count = lax.axis_size(CHAN)
    me = lax.axis_index(STN).astype(jnp.int32)
    all_channels = chan_dev * chan_count
    all_stations = row_count * stn_count

    raw = gains.reshape(chan_dev, 8 * K, row_count)
    over = [lax.ppermute(raw[f:f + 1], STN, hop_pairs(2, stn_count)) for f in range(chan_dev)]
    mate = lax.ppermute(raw, STN, hop_pairs(1, stn_count))
    far = [lax.ppermute(over[0], STN, hop_pairs(1, stn_count))]
    far.append(lax.ppermute(over[1], STN, hop_pairs(1, stn_count)))
    factor = beam_factor(beam, group_of).reshape(K, stn_count, row_count).swapaxes(0, 1)
    row_factor = lax.dynamic_index_in_dim(factor, me, 0, False)

    up = [(i, i + 1) for i in range(chan_count - 1)]
    down = [(i + 1, i) for i in range(chan_count - 1)]
    before, after = lax.ppermute(gains, CHAN, up), lax.ppermute(gains, CHAN, down)
    extended = jnp.concatenate([before, gains, after], axis=0)
    second = extended[2:] - 2.0 * extended[1:-1] + extended[:-2]
    positions = lax.axis_index(CHAN) * chan_dev - 1 + jnp.arange(chan_dev + 2, dtype=jnp.int32)
    inside = ((positions >= 1) & (positions <= all_channels - 2)).astype(F32)
    second = second * inside[:, None, None, None, None, None]
    smooth_grad = second[:-2] - 2.0 * second[1:-1] + second[2:]
    own_second = second[1:-1]
    smooth_local = jnp.sum(own_second * own_second, axis=(0, 1, 2, 3))

    sels = operands()
    me1 = me[None]
    jall0, res0, wgt0, stats = call_model(0, me1, (raw, mate, over[0], far[0]), factor, coherency, vis_data, flags, sels, None, None)
    jall1, res1, wgt1, _, spread = call_model(1, me1, (raw, mate, over[1], far[1]), factor, coherency, vis_data, flags, sels, smooth_local, stats, chan_count * stn_count)

    arrived = lax.all_to_all(spread, ALL, 0, 0, tiled=True)
    row0, *cols0 = call_grad(0, me1, jall0, coherency, res0, wgt0, sels)
    cols0 = cols0[:1] + [lax.ppermute(cols0[h], STN, hop_pairs(h, stn_count)) for h in range(1, stn_count)]
    row1, *cols1 = call_grad(1, me1, jall1, coherency, res1, wgt1, sels)
    cols1 = cols1[:1] + [lax.ppermute(cols1[h], STN, hop_pairs(h, stn_count)) for h in range(1, stn_count)]
    totals = jnp.sum(arrived, axis=0)
    sq, count, smooth = totals[0], totals[1], totals[2]

    norm_scale = all_channels * all_stations / count
    steps = []
    for f, (row, cols) in enumerate(((row0, cols0), (row1, cols1))):
        both = row + (cols[0] + cols[1]) + (cols[2] + cols[3])
        grad = both[:8 * K].reshape(2, 2, 2, K, row_count).swapaxes(0, 1)
        curv = both[8 * K:]
        gradient_f = norm_scale * row_factor * grad + smooth_weight * smooth_grad[f]
        curvature = norm_scale * row_factor * row_factor * curv + damping
        steps.append(gradient_f / curvature)
    gain_step = jnp.stack(steps)
    loss_value = (norm_scale * sq + smooth_weight * smooth) / (all_channels * all_stations)
    return gain_step, loss_value


def solution(mesh):
    parts = Mesh(mesh.devices.reshape(4, 2, 8, 4), ("chan_x", "chan_y", "chan_z", "stn"))
    in_specs = (
        P(CHAN, None, None, None, None, STN),
        P(CHAN, None, None, STN, None),
        P(CHAN, None, None, None, STN, None),
        P(CHAN, STN, None),
        P(),
        P(),
    )
    out_specs = (P(CHAN, None, None, None, None, STN), P())

    return jax.shard_map(on_device, mesh=parts, in_specs=in_specs, out_specs=out_specs, check_vma=False)
```

```python
import functools

import jax
import jax.numpy as jnp
import numpy as np
from jax import lax
from jax.experimental import pallas as pl
from jax.experimental.pallas import tpu as pltpu
from jax.sharding import Mesh
from jax.sharding import PartitionSpec as P


BF = jnp.bfloat16
F32 = jnp.float32
CHAN = ("chan_x", "chan_y", "chan_z")
STN = "stn"
ALL = ("chan_x", "chan_y", "chan_z", "stn")
smooth_weight = 0.05
damping = 0.3


def selections():
    sel_w = np.zeros((64, 16), np.float32)
    sel_l = np.zeros((2, 16, 16), np.float32)
    for s in range(2):
        for t in range(2):
            for i in range(2):
                for r in range(2):
                    kk = ((s * 2 + t) * 2 + i) * 2 + r
                    for a in range(2):
                        sel_l[a, s * 8 + r * 4 + a * 2 + i, kk] = 1.0
                        sel_w[a * 16 + kk, t * 8 + r * 4 + a * 2 + i] = 1.0
                        sel_w[32 + a * 16 + kk, t * 8 + (1 - r) * 4 + a * 2 + i] = -1.0 if r == 0 else 1.0
    sel_c = np.zeros((2, 16, 16), np.float32)
    sel_q = np.zeros((4, 16, 16), np.float32)
    for s in range(2):
        for a in range(2):
            for i in range(2):
                re, im = s * 8 + a * 2 + i, s * 8 + 4 + a * 2 + i
                sel_c[a, s * 8 + i, re] = -1.0
                sel_c[a, s * 8 + 2 + i, im] = -1.0
                sel_c[a, s * 8 + 4 + i, im] = -1.0
                sel_c[a, s * 8 + 6 + i, re] = 1.0
                for half in range(2):
                    row = s * 8 + half * 4 + i
                    sel_q[a * 2, row, re] = -1.0
                    sel_q[a * 2, row + 2, im] = -1.0
                    sel_q[a * 2 + 1, row, im] = 1.0
                    sel_q[a * 2 + 1, row + 2, re] = -1.0
    w2 = np.concatenate([sel_w, sel_q.reshape(64, 16)], axis=0)
    return w2, sel_l, sel_c.reshape(32, 16)


def operands():
    return tuple(jnp.asarray(x, BF) for x in selections())


def dot(a, b):
    return jnp.dot(a, b, preferred_element_type=F32)


def dot_t(a, b):
    return lax.dot_general(a, b, (((1,), (1,)), ((), ())), preferred_element_type=F32)


def dot_l(a, b):
    return lax.dot_general(a, b, (((0,), (0,)), ((), ())), preferred_element_type=F32)


def split(x):
    high = x.astype(BF)
    return high, (x - high.astype(F32)).astype(BF)


def parts_of(x):
    high = x.astype(BF).astype(F32)
    return jnp.concatenate([high, x - high], axis=0).astype(BF)


K = 16
ROWS = 128
LANES = 128
TILES = ROWS // 16
STEP = 2


def weights_of(first, flags, wgt, groups):
    blocks, cols = flags.shape
    rows8 = lax.broadcasted_iota(jnp.int32, (ROWS, blocks), 0) // 16 == lax.broadcasted_iota(jnp.int32, (ROWS, blocks), 1)
    wide = dot(rows8.astype(F32).astype(BF), flags.astype(F32).astype(BF)).astype(BF)
    for g in range(groups):
        at = (lax.broadcasted_iota(jnp.int32, (cols, LANES), 1) + g * LANES) // 16
        at = at == lax.broadcasted_iota(jnp.int32, (cols, LANES), 0)
        full = dot(wide, at.astype(F32).astype(BF))
        row_id = lax.broadcasted_iota(jnp.int32, (ROWS, LANES), 0) + first
        col_id = lax.broadcasted_iota(jnp.int32, (ROWS, LANES), 1) + g * LANES
        wgt[:, g * LANES:(g + 1) * LANES] = jnp.where(row_id == col_id, 0.0, full)


def in_fours(turn):
    def four(i, _):
        for n in range(4):
            turn(i * 4 + n)
        return 0

    lax.fori_loop(0, K // 4, four, 0)


def model_operands(jall, me, w2, sell, wr, wi, lr):
    groups = jall.shape[0]

    def turn(k):
        for g in range(groups):
            w = dot(w2[0:64], parts_of(jall[g, pl.ds(k, 8, stride=16), :])).astype(BF)
            for b in range(2):
                wr[k, g, :, b * 128:(b + 1) * 128] = w[b * 16:(b + 1) * 16]
                wi[k, g, :, b * 128:(b + 1) * 128] = w[32 + b * 16:48 + b * 16]
        hm = parts_of(jall[me, pl.ds(k, 8, stride=16), :])
        for a in range(2):
            l = dot_l(hm, sell[a]).astype(BF)
            for t in range(TILES):
                lr[k, t, a * 16:(a + 1) * 16, :] = l[t * 16:(t + 1) * 16]

    in_fours(turn)


def model(me_ref, own, mate, over, far, factor, coh, vis, flags, w2, sell, smooth, earlier, jall, res, wgt, stats, *rest):
    *spread, w_all, wr, wi, lr = rest
    spread = spread[0] if spread else None
    groups = jall.shape[0]
    t = pl.program_id(0)
    me = me_ref[0]

    @pl.when(t == 0)
    def _():
        for hop, piece in enumerate((own, mate, over, far)):
            g = me ^ hop
            scale = factor[g]
            for plane in range(8):
                at = slice(plane * K, (plane + 1) * K)
                jall[g, at, :] = piece[0, at, :] * scale
        weights_of(me * ROWS, flags[0], w_all, groups)
        model_operands(jall, me, w2, sell, wr, wi, lr)
        stats[...] = earlier[...]
        stats[16:32] += smooth[...]

    def tile(n, _):
        rows = pl.ds(pl.multiple_of(n * 16, 16), 16)
        at = t * STEP + n
        w_rows = w_all[pl.ds(pl.multiple_of(at * 16, 16), 16), :]
        wgt[rows, :] = w_rows
        total = jnp.zeros((16, 128), F32)
        used = jnp.zeros((16, 128), F32)
        for g in range(groups):
            cols = slice(g * 128, (g + 1) * 128)
            acc = [[[jnp.zeros((16, 128), F32)] * 2 for _ in range(2)] for _ in range(2)]
            for k in range(K):
                o_re = dot(lr[k, at], wr[k, g])
                o_im = dot(lr[k, at], wi[k, g])
                c_re = coh[0, k, 0, rows, cols].astype(F32)
                c_im = coh[0, k, 1, rows, cols].astype(F32)
                for a in range(2):
                    for b in range(2):
                        re = o_re[a * 16:(a + 1) * 16, b * 128:(b + 1) * 128]
                        im = o_im[a * 16:(a + 1) * 16, b * 128:(b + 1) * 128]
                        acc[a][b] = [acc[a][b][0] + c_re * re - c_im * im,
                                     acc[a][b][1] + c_re * im + c_im * re]
            w = w_rows[:, cols]
            used = used + w
            for a in range(2):
                for b in range(2):
                    for r in range(2):
                        v = w * (vis[0, r, a, b, rows, cols].astype(F32) - acc[a][b][r])
                        res[b, r, a, rows, cols] = v
                        total = total + v * v
        stats[0:8] += total[:8] + total[8:]
        stats[8:16] += used[:8] + used[8:]
        return 0

    lax.fori_loop(0, STEP, tile, 0)
    if spread is not None:
        @pl.when(t == pl.num_programs(0) - 1)
        def _():
            lane = lax.broadcasted_iota(jnp.int32, spread.shape, 1)
            sums = [jnp.sum(stats[lo:hi]) for lo, hi in ((0, 8), (8, 16), (16, 32))]
            spread[...] = jnp.where(lane == 0, sums[0], jnp.where(lane == 1, sums[1], jnp.where(lane == 2, sums[2], 0.0)))


def norms(x):
    return parts_of(jnp.broadcast_to(jnp.sum(x * x, axis=0, keepdims=True), (8, LANES)))


def gradient_operands(jall, me, w2, selc, lq, lc, nq, nr):
    groups = jall.shape[0]
    span = groups * LANES

    def turn(k):
        for g in range(groups):
            x = jall[g, pl.ds(k, 8, stride=16), :]
            w = dot(w2[64:128], parts_of(x)).astype(BF)
            for j in range(4):
                lq[k, :, j * span + g * 128:j * span + (g + 1) * 128] = w[j * 16:j * 16 + 16]
            nq[k, :, g * 128:(g + 1) * 128] = norms(x)
        x = jall[me, pl.ds(k, 8, stride=16), :]
        c = dot(selc[...], parts_of(x)).astype(BF)
        for a in range(2):
            lc[k, :, a * 128:(a + 1) * 128] = c[a * 16:(a + 1) * 16]
        nr[k] = norms(x)

    in_fours(turn)


def gradient(coh, wgt, res, lq, lc, nq, nr, bufs, row, col, groups, rest):
    span = groups * LANES
    halves = groups // 2

    def fill(k, t, h, y, am):
        cols = slice(h * 256, (h + 1) * 256)
        rows = slice(t * 16, (t + 1) * 16)
        c_re = coh[k, 0, rows, cols].astype(F32)
        c_im = coh[k, 1, rows, cols].astype(F32)
        for a in range(2):
            at = slice(a * ROWS + t * 16, a * ROWS + t * 16 + 16)
            for b in range(2):
                r_re = res[b, 0, a, rows, cols]
                r_im = res[b, 1, a, rows, cols]
                for r, v in ((0, c_re * r_re + c_im * r_im), (1, c_re * r_im - c_im * r_re)):
                    high, low = split(v)
                    y[b * 2 + r, h, 0, at, :] = high
                    y[b * 2 + r, h, 1, at, :] = low
        high, low = split(wgt[rows, cols] * (c_re * c_re + c_im * c_im))
        am[h, rows, :] = high
        am[h, ROWS + t * 16:ROWS + t * 16 + 16, :] = low

    top = lax.broadcasted_iota(jnp.int32, (8, 128), 0) < 4

    def reduce_part(k, j, h, s, y, cell):
        tile = y[j, h, s]
        c = dot(lc[k], tile)
        r = dot_t(lq[k, :, j * span + h * 256:j * span + (h + 1) * 256], tile)
        c = c[:8] + c[8:]
        cell[0][j, h] = c if s == 0 else cell[0][j, h] + c
        cell[1] = r if cell[1] is None else cell[1] + r

    def reduce_end(k, am, cell):
        r = cell[1][:8] + cell[1][8:]
        row[pl.ds(k, 8, stride=16), :] = jnp.where(top, r[:, :ROWS], r[:, ROWS:])
        for g in range(groups):
            h, cols = g // 2, slice(g % 2 * 128, g % 2 * 128 + 128)
            c = [cell[0][j, h][:, cols] for j in range(4)]
            t0 = c[0] + pltpu.roll(c[1], 4, 0)
            t1 = pltpu.roll(c[2], 4, 0) + c[3]
            col[g, pl.ds(k, 8, stride=16), :] = jnp.where(top, t0, t1)
        total = None
        n_row = jnp.concatenate([nr[k], nr[k]], axis=1)
        for h in range(halves):
            tile = am[h]
            cc = dot(n_row, tile)
            cc = cc[0:1] + cc[8:9]
            for g in range(2):
                col[h * 2 + g, pl.ds(128 + k, 1), :] = cc[:, g * 128:(g + 1) * 128]
            cr = dot_t(nq[k, :, h * 256:(h + 1) * 256], tile)
            cr = cr[0:1] + cr[8:9]
            cr = cr[:, :ROWS] + cr[:, ROWS:]
            total = cr if total is None else total + cr
        row[pl.ds(128 + k, 1), :] = total

    fills = [(t, h) for t in range(TILES) for h in range(halves)]
    dots = [(j, h, s) for j in range(4) for h in range(halves) for s in range(2)]
    (y0, a0), (y1, a1) = bufs
    for t, h in fills:
        fill(0, t, h, y0, a0)
    rest()

    def pair(i, _):
        for step, (y, am, y_next, am_next) in enumerate(((y0, a0, y1, a1), (y1, a1, y0, a0))):
            k = 2 * i + step
            k_next = jnp.minimum(k + 1, K - 1)
            cell = [{}, None]
            for (t, h), part in zip(fills, dots):
                reduce_part(k, *part, y, cell)
                fill(k_next, t, h, y_next, am_next)
            reduce_end(k, am, cell)
        return 0

    lax.fori_loop(0, K // 2, pair, 0)


def operand_scratch(G):
    S = G * 128
    return dict(
        model=[pltpu.VMEM((K, G, 16, 256), BF), pltpu.VMEM((K, G, 16, 256), BF), pltpu.VMEM((K, TILES, 32, 16), BF)],
        grad=[pltpu.VMEM((K, 16, 4 * S), BF), pltpu.VMEM((K, 16, 2 * ROWS), BF), pltpu.VMEM((K, 16, S), BF), pltpu.VMEM((K, 16, ROWS), BF)],
        bufs=[pltpu.VMEM((4, G // 2, 2, 2 * ROWS, 256), BF), pltpu.VMEM((G // 2, 2 * ROWS, 256), BF)] * 2,
    )


def grad_kernel(f, me_ref, jall, coh_hbm, res_hbm, wgt, w2, selc, arrived, row, col0, col1, col2, col3, sums,
                coh, res, sems, col, lq, lc, nq, nr, y0, a0, y1, a1):
    groups = jall.shape[0]
    me = me_ref[0]
    load_res = pltpu.make_async_copy(res_hbm, res, sems.at[0])
    load_first = pltpu.make_async_copy(coh_hbm.at[f, pl.ds(0, 2)], coh.at[pl.ds(0, 2)], sems.at[1])
    load_rest = pltpu.make_async_copy(coh_hbm.at[f, pl.ds(2, K - 2)], coh.at[pl.ds(2, K - 2)], sems.at[2])
    load_res.start()
    load_first.start()
    load_rest.start()
    gradient_operands(jall, me, w2, selc, lq, lc, nq, nr)
    load_res.wait()
    load_first.wait()
    gradient(coh, wgt, res, lq, lc, nq, nr, ((y0, a0), (y1, a1)), row, col, groups, load_rest.wait)
    total = jnp.sum(arrived[...], axis=0, keepdims=True)
    lane = lax.broadcasted_iota(jnp.int32, total.shape, 1)
    line = lax.broadcasted_iota(jnp.int32, sums.shape, 0)
    picked = [jnp.sum(jnp.where(lane == n, total, 0.0)) for n in range(3)]
    sums[...] = jnp.where(line == 0, picked[0], jnp.where(line == 1, picked[1], picked[2]))
    for hop, out in enumerate((col0, col1, col2, col3)):
        out[...] = col[me ^ hop]


def whole(x):
    return pl.BlockSpec(x.shape, lambda i: (0,) * x.ndim)


def spec(shape):
    return pl.BlockSpec(shape, lambda i: (0,) * len(shape))


def call_model(f, me, pieces, factor, coh, vis, flags, sels, smooth, earlier, devices=0):
    G = factor.shape[0]
    S = G * LANES
    sc = operand_scratch(G)
    outs = [((G, 8 * K, LANES), None), ((2, 2, 2, ROWS, S), 3), ((ROWS, S), 0), ((32, LANES), None)]
    if devices:
        outs.append(((devices, LANES), None))

    if earlier is None:
        earlier, smooth = jnp.zeros((32, LANES), F32), jnp.zeros((16, LANES), F32)

    operands_in = (coh, vis, flags, sels[0], sels[1])
    if f == 0:
        operands_in = tuple(pltpu.with_memory_space_constraint(x, pltpu.HBM) for x in operands_in)
        pieces = (pltpu.with_memory_space_constraint(pieces[0], pltpu.HBM), *pieces[1:])

    def piece_spec(x):
        at = f if x.shape[0] > 1 else 0
        return pl.BlockSpec((1, *x.shape[1:]), lambda i: (at, 0, 0))

    def out_spec(shape, dim):
        if dim is None:
            return spec(shape)
        block = shape[:dim] + (16 * STEP,) + shape[dim + 1:]
        return pl.BlockSpec(block, lambda i: tuple(i if d == dim else 0 for d in range(len(shape))))

    return pl.pallas_call(
        model, grid=(TILES // STEP,),
        out_shape=[jax.ShapeDtypeStruct(s, F32) for s, _ in outs],
        in_specs=[pl.BlockSpec(memory_space=pltpu.SMEM)] + [piece_spec(x) for x in pieces] + [
            whole(factor),
            pl.BlockSpec((1, K, 2, 16 * STEP, S), lambda i: (f, 0, 0, i, 0)),
            pl.BlockSpec((1, 2, 2, 2, 16 * STEP, S), lambda i: (f, 0, 0, 0, i, 0)),
            pl.BlockSpec((1, *flags.shape[1:]), lambda i: (f, 0, 0)),
            whole(sels[0]), whole(sels[1]), whole(smooth), whole(earlier),
        ],
        out_specs=[out_spec(*o) for o in outs],
        scratch_shapes=[pltpu.VMEM((ROWS, S), F32), *sc["model"]],
        cost_estimate=pl.CostEstimate(flops=8_000_000_000, bytes_accessed=10_000_000, transcendentals=0),
        compiler_params=pltpu.CompilerParams(vmem_limit_bytes=24 << 20),
    )(me, *pieces, factor, *operands_in, smooth, earlier)


def call_grad(f, me, jall, coh, res, wgt, sels, arrived):
    if f == 0:
        res, wgt = (pltpu.with_memory_space_constraint(x, pltpu.HBM) for x in (res, wgt))
    G = jall.shape[0]
    sc = operand_scratch(G)
    outs = [(9 * K, ROWS)] * 5 + [(8, LANES)]
    return pl.pallas_call(
        functools.partial(grad_kernel, f), grid=(1,),
        out_shape=[jax.ShapeDtypeStruct(s, F32) for s in outs],
        in_specs=[pl.BlockSpec(memory_space=pltpu.SMEM), whole(jall), pl.BlockSpec(memory_space=pl.ANY), pl.BlockSpec(memory_space=pl.ANY),
                  whole(wgt), whole(sels[0]), whole(sels[2]), whole(arrived)],
        out_specs=[spec(s) for s in outs],
        scratch_shapes=[pltpu.VMEM(coh.shape[1:], BF), pltpu.VMEM(res.shape, F32), pltpu.SemaphoreType.DMA((3,)),
                        pltpu.VMEM((G, 9 * K, ROWS), F32), *sc["grad"], *sc["bufs"]],
        cost_estimate=pl.CostEstimate(flops=20_000_000_000, bytes_accessed=10_000_000, transcendentals=0),
        compiler_params=pltpu.CompilerParams(vmem_limit_bytes=36 << 20),
    )(me, jall, pltpu.with_memory_space_constraint(coh, pltpu.HBM), res, wgt, sels[0], sels[2], arrived)


def beam_factor(beam, group_of):
    groups = beam.shape[0]
    onehot = (group_of[None, :] == jnp.arange(groups, dtype=jnp.int32)[:, None]).astype(F32)
    return jnp.sum(beam[:, :, None] * onehot[:, None, :], axis=0)


def hop_pairs(hop, count):
    return [(i, i ^ hop) for i in range(count)]


def on_device(gains, coherency, vis_data, flags, beam, group_of):
    chan_dev = gains.shape[0]
    row_count = gains.shape[5]
    stn_count = lax.axis_size(STN)
    chan_count = lax.axis_size(CHAN)
    me = lax.axis_index(STN).astype(jnp.int32)
    all_channels = chan_dev * chan_count
    all_stations = row_count * stn_count

    raw = gains.reshape(chan_dev, 8 * K, row_count)
    over = lax.ppermute(raw, STN, hop_pairs(2, stn_count))
    mate = lax.ppermute(raw, STN, hop_pairs(1, stn_count))
    far = lax.ppermute(over, STN, hop_pairs(1, stn_count))
    factor = beam_factor(beam, group_of).reshape(K, stn_count, row_count).swapaxes(0, 1)

    up = [(i, i + 1) for i in range(chan_count - 1)]
    down = [(i + 1, i) for i in range(chan_count - 1)]
    before, after = lax.ppermute(gains, CHAN, up), lax.ppermute(gains, CHAN, down)
    extended = jnp.concatenate([before, gains, after], axis=0)
    second = extended[2:] - 2.0 * extended[1:-1] + extended[:-2]
    positions = lax.axis_index(CHAN) * chan_dev - 1 + jnp.arange(chan_dev + 2, dtype=jnp.int32)
    inside = ((positions >= 1) & (positions <= all_channels - 2)).astype(F32)
    second = second * inside[:, None, None, None, None, None]
    smooth_grad = second[:-2] - 2.0 * second[1:-1] + second[2:]
    own_second = second[1:-1]
    smooth_local = jnp.sum(own_second * own_second, axis=(0, 1, 2, 3))

    sels = operands()
    me1 = me[None]
    jall0, res0, wgt0, stats = call_model(0, me1, (raw, mate, over, far), factor, coherency, vis_data, flags, sels, None, None)
    jall1, res1, wgt1, _, spread = call_model(1, me1, (raw, mate, over, far), factor, coherency, vis_data, flags, sels, smooth_local, stats, chan_count * stn_count)

    arrived = lax.all_to_all(spread, ALL, 0, 0, tiled=True)
    row0, *cols0, _ = call_grad(0, me1, jall0, coherency, res0, wgt0, sels, jnp.zeros((8, row_count), F32))
    cols0 = cols0[:1] + [lax.ppermute(cols0[h], STN, hop_pairs(h, stn_count)) for h in range(1, stn_count)]
    row1, *cols1, totals = call_grad(1, me1, jall1, coherency, res1, wgt1, sels, arrived)
    cols1 = cols1[:1] + [lax.ppermute(cols1[h], STN, hop_pairs(h, stn_count)) for h in range(1, stn_count)]
    late, row1 = lax.optimization_barrier((factor, row1))
    row_factor = lax.dynamic_index_in_dim(late, me, 0, False)
    norm_scale = all_channels * all_stations / totals[1]
    steps = []
    for f, (row, cols) in enumerate(((row0, cols0), (row1, cols1))):
        both = row + (cols[0] + cols[1]) + (cols[2] + cols[3])
        grad = both[:8 * K].reshape(2, 2, 2, K, row_count).swapaxes(0, 1)
        curv = both[8 * K:]
        gradient_f = norm_scale * row_factor * grad + smooth_weight * smooth_grad[f]
        curvature = norm_scale * row_factor * row_factor * curv + damping
        steps.append(gradient_f / curvature)
    gain_step = jnp.stack(steps)
    loss_value = (norm_scale[0] * totals[0, 0] + smooth_weight * totals[2, 0]) / (all_channels * all_stations)
    return gain_step, loss_value


def solution(mesh):
    parts = Mesh(mesh.devices.reshape(4, 2, 8, 4), ("chan_x", "chan_y", "chan_z", "stn"))
    in_specs = (
        P(CHAN, None, None, None, None, STN),
        P(CHAN, None, None, STN, None),
        P(CHAN, None, None, None, STN, None),
        P(CHAN, STN, None),
        P(),
        P(),
    )
    out_specs = (P(CHAN, None, None, None, None, STN), P())

    return jax.shard_map(on_device, mesh=parts, in_specs=in_specs, out_specs=out_specs, check_vma=False)
```
